256 devices in a mesh: phi: 16 (over z, core), gz: 16 (over y, x).
Axes of the slice: x: 4, y: 4, z: 8, core: 2. Of those that a mesh axis runs over, the one named last changes fastest.
Arguments:
- charge: float32 [1024, 256, 256], P('phi', 'gz'), may hold values from -24 to 24
- outer_held: int32 [256], replicated, may hold values 0 or 1
- end_held: int32 [256], replicated, may hold values 0 or 1
Outputs:
- potential: float32 [1024, 256, 256], P('phi', 'gz')
- scales: float32 [2, 1024], P(None, 'phi')
The draws below stay inside these ranges and needn't reach their ends.
Inputs may be any that keep to these rules, and one draw needn't show every extreme that they name: `outer_held`: 1 holds the boundary at zero potential, 0 leaves it without flux. `end_held`: 1 holds both z ends of the radial cell at zero potential, 0 leaves them without flux.
All inputs are finite; a program needn't handle non-finite values.
Results may differ from the reference program's by a relative error of at most 0.0003.
Values sent between devices are 32-bit elements; how exact they have to be, the bound alone decides.
A program may use at most 128 MiB of HBM per device.

```python
import math
import jax
import jax.numpy as jnp
from jax import lax

NPHI = 1024
NR = 256
VCYC = 2
NU = 2
KC = 3
RIN = 131
NZ = 256


def set_ends(array, own_key, least, largest):
    place = [jax.random.randint(jax.random.fold_in(own_key, axis), (), 0, length) for axis, length in enumerate(array.shape)]
    longest = array.shape.index(max(array.shape))
    neighbour = place[:longest] + [(place[longest] + 1) % array.shape[longest]] + place[longest + 1:]
    return array.at[tuple(place)].set(least).at[tuple(neighbour)].set(largest)


def steps_of(own_key, dims, pieces, low, largest):
    gain, own = 1.0, jax.random.fold_in(own_key, 6)
    for dim, shards_of in pieces:
        heights = jnp.exp(jax.random.uniform(jax.random.fold_in(own, dim), (shards_of,), jnp.float32, low / len(pieces), largest / len(pieces)))
        gain = gain * jnp.repeat(heights, dims[dim] // shards_of).reshape([-1 if axis == dim else 1 for axis in range(len(dims))])
    return gain


def bell_draw(own_key, shape, scale, reach, pieces=(), kind=jnp.bfloat16):
    values = jax.random.normal(own_key, shape, jnp.float32) * scale
    if len(pieces) > 0:
        values = steps_of(own_key, shape, pieces, -0.22, 0.18) * values
    return jnp.clip(values, min=-reach, max=reach).astype(kind)


def setup_inputs(seed: int = 0) -> dict:
    key_of = jax.random.split(jax.random.key(seed), 4)
    return {
        "charge": bell_draw(key_of[0], (NPHI, NZ, NR), 4.0, 24.0, ((0, 16), (1, 16)), jnp.float32),
        "outer_held": set_ends((jax.random.randint(key_of[1], (NZ,), 0, 2) < 1).astype(jnp.int32), jax.random.fold_in(key_of[1], 1), 0, 1),
        "end_held": set_ends((jax.random.randint(key_of[2], (NR,), 0, 2) < 1).astype(jnp.int32), jax.random.fold_in(key_of[2], 1), 0, 1),
    }


relaxation = 0.8
small_floor = 1e-06

def hartley_table(length):
    row_ids = lax.broadcasted_iota(jnp.int32, (length, length), 0)
    col_ids = lax.broadcasted_iota(jnp.int32, (length, length), 1)
    phases = (row_ids * col_ids % length).astype(jnp.float32) * (2.0 * math.pi / length)
    return (jnp.cos(phases) + jnp.sin(phases)) * (1.0 / math.sqrt(length))

def transform_rows(hartley, values):
    flat = values.reshape(values.shape[0], -1)
    result = jnp.dot(hartley, flat, precision=lax.Precision.HIGHEST, preferred_element_type=jnp.float32)
    return result.reshape(values.shape)

def radial_terms(radial_count, coarse):
    position = jnp.arange(radial_count, dtype=jnp.float32)
    if coarse:
        radius = RIN + 2.0 * position + 1.0
        return (radius, (radius - 1.0) / (4.0 * radius), (radius + 1.0) / (4.0 * radius), 0.25)
    radius = RIN + position + 0.5
    return (radius, (radius - 0.5) / radius, (radius + 0.5) / radius, 1.0)

def diagonal(mode_ids, axial_ids, total_axial, radial, outer_bc, end_bc):
    radius, inward, outward, axial = radial
    last_radial = radius.shape[0] - 1
    radial_ids = jnp.arange(radius.shape[0], dtype=jnp.int32)
    open_out = (radial_ids[None, :] == last_radial) & (outer_bc[:, None] == 0)
    open_low = (axial_ids[:, None] == 0) & (end_bc[None, :] == 0)
    open_high = (axial_ids[:, None] == total_axial - 1) & (end_bc[None, :] == 0)
    baseline = inward[None, :] + outward[None, :] * jnp.where(open_out, 0.0, 1.0)
    baseline = baseline + axial * (jnp.where(open_low, 0.0, 1.0) + jnp.where(open_high, 0.0, 1.0))
    mode_order = jnp.minimum(mode_ids, NPHI - mode_ids).astype(jnp.float32)
    return baseline[None] + (mode_order * mode_order)[:, None, None] / (radius * radius)[None, None, :]

def neighbours(extended, radial):
    radius, inward, outward, axial = radial
    middle = extended[:, 1:-1, :]
    zero_edge = jnp.zeros_like(middle[:, :, :1])
    below_r = jnp.concatenate([zero_edge, middle[:, :, :-1]], axis=2)
    above_r = jnp.concatenate([middle[:, :, 1:], zero_edge], axis=2)
    return axial * (extended[:, 2:, :] + extended[:, :-2, :]) + inward * below_r + outward * above_r

def relax_step(extended, source, diag_part, radial):
    middle = extended[:, 1:-1, :]
    return middle + relaxation * (source + neighbours(extended, radial) - diag_part * middle) / diag_part

def operate(extended, diag_part, radial):
    return diag_part * extended[:, 1:-1, :] - neighbours(extended, radial)

def pad_axial(values):
    return jnp.pad(values, ((0, 0), (1, 1), (0, 0)))

def restrict(residual):
    modes, cells_z, cells_r = residual.shape
    return residual.reshape(modes, cells_z // 2, 2, cells_r // 2, 2).sum(axis=(2, 4)) * 0.25

def prolong(correction):
    return jnp.repeat(jnp.repeat(correction, 2, axis=1), 2, axis=2)

def solve_block(spectrum, first_mode, outer_held, end_held):
    mode_ids = first_mode + jnp.arange(spectrum.shape[0], dtype=jnp.int32)
    fine_terms = radial_terms(NR, False)
    coarse_terms = radial_terms(NR // 2, True)
    fine_diag = diagonal(mode_ids, jnp.arange(NZ, dtype=jnp.int32), NZ, fine_terms, outer_held, end_held)
    coarse_diag = diagonal(mode_ids, jnp.arange(NZ // 2, dtype=jnp.int32), NZ // 2, coarse_terms, outer_held[0::2], end_held[0::2])
    solution = jnp.zeros_like(spectrum)
    scale_rows = []
    for cycle_index in range(VCYC):
        for sweep_index in range(NU):
            solution = relax_step(pad_axial(solution), spectrum, fine_diag, fine_terms)
        residual = spectrum - operate(pad_axial(solution), fine_diag, fine_terms)
        coarse_rhs = restrict(residual)
        estimate = relaxation * coarse_rhs / coarse_diag
        for sweep_index in range(KC):
            estimate = relax_step(pad_axial(estimate), coarse_rhs, coarse_diag, coarse_terms)
        spread = prolong(estimate)
        image = operate(pad_axial(spread), fine_diag, fine_terms)
        top = lax.optimization_barrier(jnp.sum(residual * image, axis=(1, 2)))
        bottom = lax.optimization_barrier(jnp.sum(image * image, axis=(1, 2)))
        factor = top / (bottom + small_floor)
        solution = solution + factor[:, None, None] * spread
        for sweep_index in range(NU):
            solution = relax_step(pad_axial(solution), spectrum, fine_diag, fine_terms)
        scale_rows.append(factor)
    return (solution, jnp.stack(scale_rows))

def reference(charge, outer_held, end_held):
    hartley = hartley_table(NPHI)
    spectrum = transform_rows(hartley, charge)
    mode_block = math.gcd(NPHI, 64)
    count_blocks = NPHI // mode_block
    starts = jnp.arange(count_blocks, dtype=jnp.int32) * mode_block
    blocks = spectrum.reshape(count_blocks, mode_block, NZ, NR)

    def solve_one(inputs_pair):
        return solve_block(inputs_pair[0], inputs_pair[1], outer_held, end_held)
    solution, scales = lax.map(solve_one, (blocks, starts))
    solution = solution.reshape(NPHI, NZ, NR)
    scales = jnp.transpose(scales, (1, 0, 2)).reshape(VCYC, NPHI)
    potential = transform_rows(hartley, solution)
    return (potential, scales)
```

```python
import functools
import math

import jax
import jax.numpy as jnp
import numpy as np
from jax import lax
from jax.experimental import pallas as pl
from jax.experimental.pallas import tpu as pltpu
from jax.sharding import PartitionSpec as P

NPHI = 1024
VCYC = 2
NU = 2
KC = 3
RIN = 131
NR = 256
NZ = 256
HALF = 128
FEW = 4

relaxation = 0.8
small_floor = 1e-06
f32 = jnp.float32
bf16 = jnp.bfloat16

PAD = 8
CH = 32


def hartley_tables():
    k = np.arange(NPHI)
    phase = (np.outer(k, k) % NPHI) * (2.0 * math.pi / NPHI)
    table = ((np.cos(phase) + np.sin(phase)) / math.sqrt(NPHI)).astype(np.float32)
    high = table.astype(jnp.bfloat16)
    low = (table - high.astype(np.float32)).astype(jnp.bfloat16)
    return high, low


def parity_table():
    perm = np.zeros((NR, NR), np.float32)
    i = np.arange(NR)
    perm[i, (i % 2) * HALF + i // 2] = 1.0
    return perm.astype(jnp.bfloat16)


def split(values):
    high = values.astype(bf16)
    low = (values - high.astype(f32)).astype(bf16)
    return high, low


def transform_kernel(high_ref, low_ref, perm_ref, x_ref, o_ref, xh, xl):
    for piece in range(4):
        rows = pl.ds(piece * 256, 256)
        h, l = split(x_ref[rows, :])
        xh[rows, :] = jnp.dot(h, perm_ref[...], preferred_element_type=f32).astype(bf16)
        xl[rows, :] = jnp.dot(l, perm_ref[...], preferred_element_type=f32).astype(bf16)
    for piece in range(4):
        rows = pl.ds(piece * 256, 256)
        acc = jnp.dot(high_ref[rows, :], xh[...], preferred_element_type=f32)
        acc += jnp.dot(high_ref[rows, :], xl[...], preferred_element_type=f32)
        acc += jnp.dot(low_ref[rows, :], xh[...], preferred_element_type=f32)
        o_ref[rows, :] = acc


def transform(high, low, perm, x):
    return pl.pallas_call(
        transform_kernel,
        out_shape=jax.ShapeDtypeStruct((NPHI, NR), f32),
        scratch_shapes=[pltpu.VMEM((NPHI, NR), bf16), pltpu.VMEM((NPHI, NR), bf16)],
        compiler_params=pltpu.CompilerParams(vmem_limit_bytes=32 << 20),
        cost_estimate=pl.CostEstimate(
            flops=6 * NPHI * NPHI * NR, bytes_accessed=6 << 20, transcendentals=0
        ),
        name="transform",
    )(high, low, perm, x)


def lane_ids(rows=1):
    return lax.broadcasted_iota(jnp.int32, (rows, HALF), 1)


def fine_rows(parity):
    i = 2 * lane_ids() + parity
    radius = i.astype(f32) + (RIN + 0.5)
    inward = (radius - 0.5) / radius
    outward = (radius + 0.5) / radius
    return radius, inward, outward


def coarse_rows():
    radius = 2.0 * lane_ids().astype(f32) + (RIN + 1.0)
    inward = (radius - 1.0) / (4.0 * radius)
    outward = (radius + 1.0) / (4.0 * radius)
    return radius, inward, outward


def as_column(row):
    square = jnp.broadcast_to(row, (HALF, HALF))
    diag = lax.broadcasted_iota(jnp.int32, (HALF, HALF), 0) == lane_ids(HALF)
    return jnp.sum(jnp.where(diag, square, 0.0), axis=1, keepdims=True)


def setup_base(base_ref, outer_rows, end_rows):
    y = lax.broadcasted_iota(jnp.int32, (HALF, HALF), 0)
    j = lane_ids(HALF)
    for zp in range(2):
        open_outer = 1.0 - as_column(outer_rows[zp])
        for ip in range(2):
            _, inward, outward = fine_rows(ip)
            open_end = 1.0 - end_rows[ip]
            value = jnp.broadcast_to(inward + outward + 2.0, (HALF, HALF))
            if ip == 1:
                value = value - jnp.where(j == HALF - 1, outward * open_outer, 0.0)
            edge = 0 if zp == 0 else HALF - 1
            value = value - jnp.where(y == edge, open_end, 0.0)
            base_ref[2 * zp + ip] = value
    _, inward, outward = coarse_rows()
    open_outer = 1.0 - as_column(outer_rows[0])
    open_end = 1.0 - end_rows[0]
    value = jnp.broadcast_to(inward + outward + 0.5, (HALF, HALF))
    value = value - jnp.where(j == HALF - 1, outward * open_outer, 0.0)
    value = value - jnp.where((y == 0) | (y == HALF - 1), 0.25 * open_end, 0.0)
    base_ref[4] = value


def left_of(value):
    return pltpu.roll(value, 1, 1)


def right_of(value):
    return pltpu.roll(value, HALF - 1, 1)


def solve_mode(mode, f_ref, base_ref, d_ref, w_ref, va, vb, r_ref, ca, cb, cr_ref, write):
    order = jnp.minimum(mode, NPHI - mode).astype(f32)
    square = order * order
    rows_e = fine_rows(0)
    rows_o = fine_rows(1)
    first = lane_ids() == 0
    last = lane_ids() == HALF - 1
    in_e = jnp.where(first, 0.0, rows_e[1])
    out_e = rows_e[2]
    in_o = rows_o[1]
    out_o = jnp.where(last, 0.0, rows_o[2])
    radius_c, in_c0, out_c0 = coarse_rows()
    in_c = jnp.where(first, 0.0, in_c0)
    out_c = jnp.where(last, 0.0, out_c0)
    term_e = square / (rows_e[0] * rows_e[0])
    term_o = square / (rows_o[0] * rows_o[0])
    term_c = square / (radius_c * radius_c)
    chunks = [pl.ds(s, CH) for s in range(0, HALF, CH)]
    padded = [pl.ds(PAD + s, CH) for s in range(0, HALF, CH)]
    above = [pl.ds(PAD + s - 1, CH) for s in range(0, HALF, CH)]
    below = [pl.ds(PAD + s + 1, CH) for s in range(0, HALF, CH)]
    count = len(chunks)

    def neighbours(v, c):
        ee, eo, oe, oo = (v[q, padded[c], :] for q in range(4))
        oe_up, oo_up = v[2, above[c], :], v[3, above[c], :]
        ee_dn, eo_dn = v[0, below[c], :], v[1, below[c], :]
        n_ee = (oe_up + oe) + (in_e * left_of(eo) + out_e * eo)
        n_eo = (oo_up + oo) + (in_o * ee + out_o * right_of(ee))
        n_oe = (ee + ee_dn) + (in_e * left_of(oo) + out_e * oo)
        n_oo = (eo + eo_dn) + (in_o * oe + out_o * right_of(oe))
        return (ee, eo, oe, oo), (n_ee, n_eo, n_oe, n_oo)

    def sweep(src, dst, emit=None):
        for c in range(count):
            centre, near = neighbours(src, c)
            for q in range(4):
                value = (1.0 - relaxation) * centre[q] + w_ref[q, chunks[c], :] * (
                    f_ref[q, chunks[c], :] + near[q]
                )
                if emit is None:
                    dst[q, padded[c], :] = value
                else:
                    emit(q, c * CH, value)

    for c in range(count):
        for q in range(4):
            d = base_ref[q, chunks[c], :] + (term_e if q % 2 == 0 else term_o)
            w = relaxation / d
            d_ref[q, chunks[c], :] = d
            w_ref[q, chunks[c], :] = w
            va[q, padded[c], :] = w * f_ref[q, chunks[c], :]
        d_ref[4, chunks[c], :] = relaxation / (base_ref[4, chunks[c], :] + term_c)

    factors = []
    cur, other = va, vb
    for cycle in range(VCYC):
        for s in range(1 if cycle == 0 else 0, NU):
            sweep(cur, other)
            cur, other = other, cur
        for c in range(count):
            centre, near = neighbours(cur, c)
            total = None
            for q in range(4):
                res = f_ref[q, chunks[c], :] + near[q] - d_ref[q, chunks[c], :] * centre[q]
                r_ref[q, chunks[c], :] = res
                total = res if total is None else total + res
            total = total * 0.25
            cr_ref[chunks[c], :] = total
            ca[padded[c], :] = d_ref[4, chunks[c], :] * total
        now, later = ca, cb
        for s in range(KC):
            for c in range(count):
                w = now[padded[c], :]
                near = (
                    in_c * left_of(w)
                    + out_c * right_of(w)
                    + 0.25 * (now[above[c], :] + now[below[c], :])
                )
                later[padded[c], :] = (1.0 - relaxation) * w + d_ref[4, chunks[c], :] * (
                    cr_ref[chunks[c], :] + near
                )
            now, later = later, now
        top = jnp.zeros((8, HALF), f32)
        bottom = jnp.zeros((8, HALF), f32)
        for c in range(count):
            w = now[padded[c], :]
            low_e = in_e * left_of(w) + out_e * w
            low_o = in_o * w + out_o * right_of(w)
            up = now[above[c], :] + w
            down = now[below[c], :] + w
            for q in range(4):
                image = d_ref[q, chunks[c], :] * w - (low_e if q % 2 == 0 else low_o)
                image = image - (up if q < 2 else down)
                res = r_ref[q, chunks[c], :]
                for g in range(CH // 8):
                    part = image[8 * g : 8 * g + 8]
                    top = top + res[8 * g : 8 * g + 8] * part
                    bottom = bottom + part * part
        factor = jnp.sum(top, keepdims=True) / (jnp.sum(bottom, keepdims=True) + small_floor)
        factors.append(factor)
        for c in range(count):
            add = factor * now[padded[c], :]
            for q in range(4):
                cur[q, padded[c], :] = cur[q, padded[c], :] + add
        for s in range(NU):
            if cycle == VCYC - 1 and s == NU - 1:
                sweep(cur, None, write)
            else:
                sweep(cur, other)
                cur, other = other, cur
    return factors


def solve_kernel(outer_ref, end_ref, perm_ref, f_ref, o_ref, s_ref, f, base, d, w, va, vb, r, ca, cb, cr, flat):
    step = pl.program_id(0)

    @pl.when(step == 0)
    def _():
        held = jnp.concatenate([outer_ref[...], end_ref[...]], axis=0).astype(f32).astype(bf16)
        held = jnp.concatenate([held] * 8, axis=0)
        held = jnp.dot(held, perm_ref[...], preferred_element_type=f32)
        outer_rows = [held[0:1, :HALF], held[0:1, HALF:]]
        end_rows = [held[1:2, :HALF], held[1:2, HALF:]]
        setup_base(base, outer_rows, end_rows)
        for ref in (va, vb):
            ref[:, 0:PAD, :] = jnp.zeros((4, PAD, HALF), f32)
            ref[:, HALF + PAD :, :] = jnp.zeros((4, PAD, HALF), f32)
        for ref in (ca, cb):
            ref[0:PAD, :] = jnp.zeros((PAD, HALF), f32)
            ref[HALF + PAD :, :] = jnp.zeros((PAD, HALF), f32)

    mode = (lax.axis_index("phi") * 16 + lax.axis_index("gz")) * FEW + step
    for ip in range(2):
        flat[ip] = f_ref[0, :, ip * HALF : (ip + 1) * HALF]
    for q in range(4):
        f[q] = flat[q % 2, pl.ds(q // 2, HALF, stride=2), :]

    def write(q, start, value):
        flat[q % 2, pl.ds(2 * start + q // 2, CH, stride=2), :] = value

    factors = solve_mode(mode, f, base, d, w, va, vb, r, ca, cb, cr, write)
    for ip in range(2):
        o_ref[0, :, ip * HALF : (ip + 1) * HALF] = flat[ip]
    for cycle in range(VCYC):
        s_ref[0, cycle : cycle + 1, :] = jnp.broadcast_to(factors[cycle], (1, HALF))


def solve(outer, end, perm, own):
    quad = lambda n: pltpu.VMEM((n, HALF, HALF), f32)
    return pl.pallas_call(
        solve_kernel,
        grid=(FEW,),
        out_shape=(
            jax.ShapeDtypeStruct((FEW, NZ, NR), f32),
            jax.ShapeDtypeStruct((FEW, 8, HALF), f32),
        ),
        in_specs=[
            pl.BlockSpec((1, NZ), lambda m: (0, 0)),
            pl.BlockSpec((1, NR), lambda m: (0, 0)),
            pl.BlockSpec((NR, NR), lambda m: (0, 0)),
            pl.BlockSpec((1, NZ, NR), lambda m: (m, 0, 0)),
        ],
        out_specs=(
            pl.BlockSpec((1, NZ, NR), lambda m: (m, 0, 0)),
            pl.BlockSpec((1, 8, HALF), lambda m: (m, 0, 0)),
        ),
        scratch_shapes=[
            quad(4), quad(5), quad(5), quad(4),
            pltpu.VMEM((4, HALF + 2 * PAD, HALF), f32),
            pltpu.VMEM((4, HALF + 2 * PAD, HALF), f32),
            quad(4),
            pltpu.VMEM((HALF + 2 * PAD, HALF), f32),
            pltpu.VMEM((HALF + 2 * PAD, HALF), f32),
            pltpu.VMEM((HALF, HALF), f32),
            pltpu.VMEM((2, NZ, HALF), f32),
        ],
        compiler_params=pltpu.CompilerParams(vmem_limit_bytes=32 << 20),
        cost_estimate=pl.CostEstimate(
            flops=200 * FEW * NZ * NR, bytes_accessed=2 << 20, transcendentals=0
        ),
        name="solve",
    )(outer, end, perm, own)


def body(tables, charge, outer_held, end_held):
    high, low, forward, backward = (jnp.asarray(t) for t in tables)
    rows = lax.all_to_all(charge, "phi", split_axis=1, concat_axis=0, tiled=True)
    spectrum = transform(high, low, forward, rows.reshape(NPHI, NR)).reshape(NPHI, 1, NR)
    spectrum = lax.all_to_all(spectrum, "phi", split_axis=0, concat_axis=1, tiled=True)
    own = lax.all_to_all(spectrum, "gz", split_axis=0, concat_axis=1, tiled=True)
    outer = outer_held.reshape(1, NZ)
    end = end_held.reshape(1, NR)
    local, scale_rows = solve(outer, end, forward, own)
    mine = jnp.transpose(scale_rows[:, :VCYC, 0])
    scales = lax.all_gather(mine, "gz", axis=1, tiled=True)
    back = lax.all_to_all(local, "gz", split_axis=1, concat_axis=0, tiled=True)
    back = lax.all_to_all(back, "phi", split_axis=1, concat_axis=0, tiled=True)
    rows_back = transform(high, low, backward, back.reshape(NPHI, NR)).reshape(NPHI, 1, NR)
    potential = lax.all_to_all(rows_back, "phi", split_axis=0, concat_axis=1, tiled=True)
    return (potential, scales)


def solution(mesh):
    in_specs = (P("phi", "gz", None), P(), P())
    out_specs = (P("phi", "gz", None), P(None, "phi"))
    high, low = hartley_tables()
    perm = parity_table()
    tables = (high, low, perm, np.ascontiguousarray(perm.T))
    return jax.shard_map(
        functools.partial(body, tables), mesh=mesh, in_specs=in_specs, out_specs=out_specs, check_vma=False
    )
```

```python
import functools
import math

import jax
import jax.numpy as jnp
import numpy as np
from jax import lax
from jax.experimental import pallas as pl
from jax.experimental.pallas import tpu as pltpu
from jax.sharding import PartitionSpec as P

NPHI = 1024
VCYC = 2
NU = 2
KC = 3
RIN = 131
NR = 256
NZ = 256
HALF = 128
FEW = 4
GROUP = 16
BLOCK = 64
MESH = pl.DeviceIdType.MESH

relaxation = 0.8
small_floor = 1e-06
f32 = jnp.float32
bf16 = jnp.bfloat16

PAD = 8
CH = 32


def hartley_tables():
    k = np.arange(NPHI)
    phase = (np.outer(k, k) % NPHI) * (2.0 * math.pi / NPHI)
    table = ((np.cos(phase) + np.sin(phase)) / math.sqrt(NPHI)).astype(np.float32)
    order = k.reshape(GROUP, GROUP, FEW).transpose(1, 0, 2).reshape(-1)
    table = table[order]
    high = table.astype(jnp.bfloat16)
    low = (table - high.astype(np.float32)).astype(jnp.bfloat16)
    return high, low, np.ascontiguousarray(high.T), np.ascontiguousarray(low.T)


def parity_table():
    perm = np.zeros((NR, NR), np.float32)
    i = np.arange(NR)
    perm[i, (i % 2) * HALF + i // 2] = 1.0
    return perm.astype(jnp.bfloat16)


def split(values):
    high = values.astype(bf16)
    low = (values - high.astype(f32)).astype(bf16)
    return high, low


def lane_ids(rows=1):
    return lax.broadcasted_iota(jnp.int32, (rows, HALF), 1)


def fine_rows(parity):
    i = 2 * lane_ids() + parity
    radius = i.astype(f32) + (RIN + 0.5)
    inward = (radius - 0.5) / radius
    outward = (radius + 0.5) / radius
    return radius, inward, outward


def coarse_rows():
    radius = 2.0 * lane_ids().astype(f32) + (RIN + 1.0)
    inward = (radius - 1.0) / (4.0 * radius)
    outward = (radius + 1.0) / (4.0 * radius)
    return radius, inward, outward


def as_column(row):
    square = jnp.broadcast_to(row, (HALF, HALF))
    diag = lax.broadcasted_iota(jnp.int32, (HALF, HALF), 0) == lane_ids(HALF)
    return jnp.sum(jnp.where(diag, square, 0.0), axis=1, keepdims=True)


def setup_base(base_ref, outer_rows, end_rows):
    y = lax.broadcasted_iota(jnp.int32, (HALF, HALF), 0)
    j = lane_ids(HALF)
    for zp in range(2):
        open_outer = 1.0 - as_column(outer_rows[zp])
        for ip in range(2):
            _, inward, outward = fine_rows(ip)
            open_end = 1.0 - end_rows[ip]
            value = jnp.broadcast_to(inward + outward + 2.0, (HALF, HALF))
            if ip == 1:
                value = value - jnp.where(j == HALF - 1, outward * open_outer, 0.0)
            edge = 0 if zp == 0 else HALF - 1
            value = value - jnp.where(y == edge, open_end, 0.0)
            base_ref[2 * zp + ip] = value
    _, inward, outward = coarse_rows()
    open_outer = 1.0 - as_column(outer_rows[0])
    open_end = 1.0 - end_rows[0]
    value = jnp.broadcast_to(inward + outward + 0.5, (HALF, HALF))
    value = value - jnp.where(j == HALF - 1, outward * open_outer, 0.0)
    value = value - jnp.where((y == 0) | (y == HALF - 1), 0.25 * open_end, 0.0)
    base_ref[4] = value


def left_of(value):
    return pltpu.roll(value, 1, 1)


def right_of(value):
    return pltpu.roll(value, HALF - 1, 1)


def solve_mode(mode, f_ref, base_ref, d_ref, w_ref, va, vb, r_ref, ca, cb, cr_ref, write):
    order = jnp.minimum(mode, NPHI - mode).astype(f32)
    square = order * order
    rows_e = fine_rows(0)
    rows_o = fine_rows(1)
    first = lane_ids() == 0
    last = lane_ids() == HALF - 1
    in_e = jnp.where(first, 0.0, rows_e[1])
    out_e = rows_e[2]
    in_o = rows_o[1]
    out_o = jnp.where(last, 0.0, rows_o[2])
    radius_c, in_c0, out_c0 = coarse_rows()
    in_c = jnp.where(first, 0.0, in_c0)
    out_c = jnp.where(last, 0.0, out_c0)
    term_e = square / (rows_e[0] * rows_e[0])
    term_o = square / (rows_o[0] * rows_o[0])
    term_c = square / (radius_c * radius_c)
    chunks = [pl.ds(s, CH) for s in range(0, HALF, CH)]
    padded = [pl.ds(PAD + s, CH) for s in range(0, HALF, CH)]
    above = [pl.ds(PAD + s - 1, CH) for s in range(0, HALF, CH)]
    below = [pl.ds(PAD + s + 1, CH) for s in range(0, HALF, CH)]
    count = len(chunks)

    def neighbours(v, c):
        ee, eo, oe, oo = (v[q, padded[c], :] for q in range(4))
        oe_up, oo_up = v[2, above[c], :], v[3, above[c], :]
        ee_dn, eo_dn = v[0, below[c], :], v[1, below[c], :]
        n_ee = (oe_up + oe) + (in_e * left_of(eo) + out_e * eo)
        n_eo = (oo_up + oo) + (in_o * ee + out_o * right_of(ee))
        n_oe = (ee + ee_dn) + (in_e * left_of(oo) + out_e * oo)
        n_oo = (eo + eo_dn) + (in_o * oe + out_o * right_of(oe))
        return (ee, eo, oe, oo), (n_ee, n_eo, n_oe, n_oo)

    def sweep(src, dst, emit=None):
        for c in range(count):
            centre, near = neighbours(src, c)
            for q in range(4):
                value = (1.0 - relaxation) * centre[q] + w_ref[q, chunks[c], :] * (
                    f_ref[q, chunks[c], :] + near[q]
                )
                if emit is None:
                    dst[q, padded[c], :] = value
                else:
                    emit(q, c * CH, value)

    for c in range(count):
        for q in range(4):
            d = base_ref[q, chunks[c], :] + (term_e if q % 2 == 0 else term_o)
            w = relaxation / d
            d_ref[q, chunks[c], :] = d
            w_ref[q, chunks[c], :] = w
            va[q, padded[c], :] = w * f_ref[q, chunks[c], :]
        d_ref[4, chunks[c], :] = relaxation / (base_ref[4, chunks[c], :] + term_c)

    factors = []
    cur, other = va, vb
    for cycle in range(VCYC):
        for s in range(1 if cycle == 0 else 0, NU):
            sweep(cur, other)
            cur, other = other, cur
        for c in range(count):
            centre, near = neighbours(cur, c)
            total = None
            for q in range(4):
                res = f_ref[q, chunks[c], :] + near[q] - d_ref[q, chunks[c], :] * centre[q]
                r_ref[q, chunks[c], :] = res
                total = res if total is None else total + res
            total = total * 0.25
            cr_ref[chunks[c], :] = total
            ca[padded[c], :] = d_ref[4, chunks[c], :] * total
        now, later = ca, cb
        for s in range(KC):
            for c in range(count):
                w = now[padded[c], :]
                near = (
                    in_c * left_of(w)
                    + out_c * right_of(w)
                    + 0.25 * (now[above[c], :] + now[below[c], :])
                )
                later[padded[c], :] = (1.0 - relaxation) * w + d_ref[4, chunks[c], :] * (
                    cr_ref[chunks[c], :] + near
                )
            now, later = later, now
        top = jnp.zeros((8, HALF), f32)
        bottom = jnp.zeros((8, HALF), f32)
        for c in range(count):
            w = now[padded[c], :]
            low_e = in_e * left_of(w) + out_e * w
            low_o = in_o * w + out_o * right_of(w)
            up = now[above[c], :] + w
            down = now[below[c], :] + w
            for q in range(4):
                image = d_ref[q, chunks[c], :] * w - (low_e if q % 2 == 0 else low_o)
                image = image - (up if q < 2 else down)
                res = r_ref[q, chunks[c], :]
                for g in range(CH // 8):
                    part = image[8 * g : 8 * g + 8]
                    top = top + res[8 * g : 8 * g + 8] * part
                    bottom = bottom + part * part
        factor = jnp.sum(top, keepdims=True) / (jnp.sum(bottom, keepdims=True) + small_floor)
        factors.append(factor)
        for c in range(count):
            add = factor * now[padded[c], :]
            for q in range(4):
                cur[q, padded[c], :] = cur[q, padded[c], :] + add
        for s in range(NU):
            if cycle == VCYC - 1 and s == NU - 1:
                sweep(cur, None, write)
            else:
                sweep(cur, other)
                cur, other = other, cur
    return factors


def block(index):
    return pl.ds(pl.multiple_of(index * BLOCK, BLOCK), BLOCK)


def peers(me, action):
    def step(o, carry):
        action(lax.rem(me + o, GROUP))
        return carry

    lax.fori_loop(1, GROUP, step, 0)


class Exchange:
    def __init__(self, axis, src, dst, send, recv):
        self.axis, self.src, self.dst, self.send, self.recv = axis, src, dst, send, recv
        self.me = lax.axis_index(axis)

    def copy(self, par, t, slot):
        return pltpu.make_async_remote_copy(
            src_ref=self.src.at[par, block(t)],
            dst_ref=self.dst.at[par, block(slot)],
            send_sem=self.send.at[par, t],
            recv_sem=self.recv.at[par, slot],
            device_id={self.axis: t},
            device_id_type=MESH,
        )

    def start(self, par, t):
        self.copy(par, t, self.me).start()

    def start_all(self, par):
        peers(self.me, lambda t: self.start(par, t))

    def keep(self, par):
        self.dst[par, block(self.me), :] = self.src[par, block(self.me), :]

    def wait_recv(self, par):
        peers(self.me, lambda t: self.copy(par, t, t).wait_recv())

    def wait_send(self, par):
        peers(self.me, lambda t: self.copy(par, t, self.me).wait_send())


def hartley(high, low, src, par, xs, exchange):
    for piece in range(4):
        rows = pl.ds(piece * 256, 256)
        h, l = split(src[par, rows, :])
        xs[rows, :HALF] = h
        xs[rows, HALF:] = l
    me = exchange.me

    def step(n, carry):
        piece = lax.rem(me // 4 + n, 4)
        rows = pl.ds(pl.multiple_of(piece * 256, 256), 256)
        both = jnp.dot(high[rows, :], xs[...], preferred_element_type=f32)
        rest = jnp.dot(low[rows, :], xs[:, :HALF], preferred_element_type=f32)
        exchange.src[par, rows, :] = both[:, :HALF] + (both[:, HALF:] + rest)
        for j in range(4):
            t = piece * 4 + lax.rem(me + j, 4)

            @pl.when(t != me)
            def _():
                exchange.start(par, t)

        return carry

    lax.fori_loop(0, 4, step, 0)


def main_kernel(
    charge_ref, outer_ref, end_ref, perm_ref, fh_ref, fl_ref, bh_ref, bl_ref,
    w_ref, s_ref,
    xin, xp, t1, r1, s1, r2, r3, r4, o4, p3, p2, q1, v1, xs,
    fh, fl, bh, bl,
    f, base, d, w, va, vb, r, ca, cb, cr, sc_src, sc,
    in_sem, table_sem, keep_sem, send, recv, sc_send, sc_recv,
):
    phi, gz = lax.axis_index("phi"), lax.axis_index("gz")
    load = pltpu.make_async_copy(charge_ref, xin, in_sem)
    load.start()
    tables = [
        pltpu.make_async_copy(src, dst, table_sem.at[n])
        for n, (src, dst) in enumerate(((fh_ref, fh), (fl_ref, fl), (bh_ref, bh), (bl_ref, bl)))
    ]
    for copy in tables:
        copy.start()
    barrier = pltpu.get_barrier_semaphore()
    for axis, me in (("phi", phi), ("gz", gz)):
        peers(
            me,
            lambda t: pl.semaphore_signal(barrier, inc=1, device_id={axis: t}, device_id_type=MESH),
        )

    first = Exchange("phi", t1, r1, send.at[0], recv.at[0])
    second = Exchange("gz", s1, r2, send.at[1], recv.at[1])
    third = Exchange("phi", r3, r4, send.at[2], recv.at[2])
    fourth = Exchange("phi", o4, p3, send.at[3], recv.at[3])
    fifth = Exchange("gz", p2, q1, send.at[4], recv.at[4])
    sixth = Exchange("phi", v1, w_ref, send.at[5], recv.at[5])

    load.wait()
    for piece in range(4):
        rows = pl.ds(piece * 256, 256)
        h, l = split(xin[piece * 16 : (piece + 1) * 16].reshape(256, NR))
        value = jnp.dot(h, perm_ref[...], preferred_element_type=f32) + jnp.dot(
            l, perm_ref[...], preferred_element_type=f32
        )
        xp[0, rows, :] = value[:, :HALF]
        xp[1, rows, :] = value[:, HALF:]
    for par in range(2):
        for z in range(GROUP):
            t1[par, z * BLOCK : (z + 1) * BLOCK, :] = xp[par, pl.ds(z, BLOCK, stride=GROUP), :]
    pl.semaphore_wait(barrier, 2 * (GROUP - 1))

    first.start_all(0)
    first.start_all(1)
    first.keep(0)
    first.keep(1)

    held = jnp.concatenate([outer_ref[...], end_ref[...]], axis=0).astype(f32).astype(bf16)
    held = jnp.concatenate([held] * 8, axis=0)
    held = jnp.dot(held, perm_ref[...], preferred_element_type=f32)
    setup_base(base, [held[0:1, :HALF], held[0:1, HALF:]], [held[1:2, :HALF], held[1:2, HALF:]])
    for ref in (va, vb):
        ref[:, 0:PAD, :] = jnp.zeros((4, PAD, HALF), f32)
        ref[:, HALF + PAD :, :] = jnp.zeros((4, PAD, HALF), f32)
    for ref in (ca, cb):
        ref[0:PAD, :] = jnp.zeros((PAD, HALF), f32)
        ref[HALF + PAD :, :] = jnp.zeros((PAD, HALF), f32)
    sc_src[...] = jnp.zeros((8, HALF), f32)
    for copy in tables:
        copy.wait()

    for par in range(2):
        first.wait_recv(par)
        hartley(fh, fl, r1, par, xs, second)
        second.keep(par)
        second.wait_recv(par)
        for b in range(GROUP):
            r3[par, pl.ds(b, BLOCK, stride=GROUP), :] = r2[par, b * BLOCK : (b + 1) * BLOCK, :]
        third.start_all(par)
        third.keep(par)

    third.wait_recv(0)
    third.wait_recv(1)

    def solve_step(m, carry):
        mode = (phi * GROUP + gz) * FEW + m
        for q in range(4):
            for b in range(GROUP):
                f[q, 8 * b : 8 * b + 8, :] = r4[
                    q % 2, pl.ds((q // 2) * BLOCK + m * GROUP + b, 8, stride=HALF), :
                ]

        def write(q, start, value):
            for g in range(CH // 8):
                b = start // 8 + g
                o4[q % 2, pl.ds((q // 2) * BLOCK + m * GROUP + b, 8, stride=HALF), :] = value[
                    8 * g : 8 * g + 8
                ]

        factors = solve_mode(mode, f, base, d, w, va, vb, r, ca, cb, cr, write)
        row_ids = lax.broadcasted_iota(jnp.int32, (8, HALF), 0)
        lanes = lane_ids(8)
        for cycle in range(VCYC):
            here = (row_ids == cycle) & (lanes == gz * FEW + m)
            sc_src[...] = sc_src[...] + jnp.where(here, factors[cycle], 0.0)
        return carry

    lax.fori_loop(0, FEW, solve_step, 0)

    fourth.start_all(0)
    fourth.start_all(1)
    fourth.keep(0)
    fourth.keep(1)

    def scale_copy(t, slot):
        return pltpu.make_async_remote_copy(
            src_ref=sc_src,
            dst_ref=sc.at[slot],
            send_sem=sc_send.at[t],
            recv_sem=sc_recv.at[slot],
            device_id={"gz": t},
            device_id_type=MESH,
        )

    peers(gz, lambda t: scale_copy(t, gz).start())
    sc[gz] = sc_src[...]

    for par in range(2):
        fourth.wait_recv(par)
        for b in range(GROUP):
            p2[par, b * BLOCK : (b + 1) * BLOCK, :] = p3[par, pl.ds(b, BLOCK, stride=GROUP), :]
        fifth.start_all(par)
        fifth.keep(par)
        fifth.wait_recv(par)
        hartley(bh, bl, q1, par, xs, sixth)
        pltpu.make_async_copy(
            v1.at[par, block(phi)], w_ref.at[par, block(phi)], keep_sem.at[par]
        ).start()

    peers(gz, lambda t: scale_copy(t, t).wait_recv())
    total = sc[0]
    for n in range(1, GROUP):
        total = total + sc[n]
    s_ref[...] = total[:VCYC, :BLOCK]

    for exchange in (first, second, third, fourth, fifth):
        for par in range(2):
            exchange.wait_send(par)
    peers(gz, lambda t: scale_copy(t, gz).wait_send())
    for par in range(2):
        sixth.wait_recv(par)
        sixth.wait_send(par)
        pltpu.make_async_copy(
            v1.at[par, block(phi)], w_ref.at[par, block(phi)], keep_sem.at[par]
        ).wait()


def run(charge, outer, end, tables):
    rows = lambda: pltpu.VMEM((2, NPHI, HALF), f32)
    quad = lambda n: pltpu.VMEM((n, HALF, HALF), f32)
    table = lambda: pltpu.VMEM((NPHI, NPHI), bf16)
    whole = pl.BlockSpec(memory_space=pltpu.VMEM)
    away = pl.BlockSpec(memory_space=pl.ANY)
    return pl.pallas_call(
        main_kernel,
        out_shape=(
            jax.ShapeDtypeStruct((2, NPHI, HALF), f32),
            jax.ShapeDtypeStruct((VCYC, BLOCK), f32),
        ),
        in_specs=[away, whole, whole, whole, away, away, away, away],
        out_specs=(away, whole),
        scratch_shapes=[
            pltpu.VMEM((BLOCK, GROUP, NR), f32),
            *[rows() for _ in range(12)],
            pltpu.VMEM((NPHI, NR), bf16),
            table(), table(), table(), table(),
            quad(4), quad(5), quad(5), quad(4),
            pltpu.VMEM((4, HALF + 2 * PAD, HALF), f32),
            pltpu.VMEM((4, HALF + 2 * PAD, HALF), f32),
            quad(4),
            pltpu.VMEM((HALF + 2 * PAD, HALF), f32),
            pltpu.VMEM((HALF + 2 * PAD, HALF), f32),
            pltpu.VMEM((HALF, HALF), f32),
            pltpu.VMEM((8, HALF), f32),
            pltpu.VMEM((GROUP, 8, HALF), f32),
            pltpu.SemaphoreType.DMA,
            pltpu.SemaphoreType.DMA((4,)),
            pltpu.SemaphoreType.DMA((2,)),
            pltpu.SemaphoreType.DMA((6, 2, GROUP)),
            pltpu.SemaphoreType.DMA((6, 2, GROUP)),
            pltpu.SemaphoreType.DMA((GROUP,)),
            pltpu.SemaphoreType.DMA((GROUP,)),
        ],
        compiler_params=pltpu.CompilerParams(
            collective_id=0, has_side_effects=True, vmem_limit_bytes=48 << 20
        ),
        name="modes",
    )(charge, outer, end, *tables)


def finish_kernel(perm_ref, w_ref, o_ref, rows):
    for z in range(0, GROUP, 4):
        flat = jnp.concatenate(
            [w_ref[0, z : z + 4].reshape(4 * GROUP, HALF), w_ref[1, z : z + 4].reshape(4 * GROUP, HALF)],
            axis=1,
        )
        h, l = split(flat)
        value = jnp.dot(h, perm_ref[...], preferred_element_type=f32) + jnp.dot(
            l, perm_ref[...], preferred_element_type=f32
        )
        for g in range(4):
            for half in range(2):
                rows[half, pl.ds(z + g, GROUP, stride=GROUP), :] = value[
                    g * GROUP : (g + 1) * GROUP, half * HALF : (half + 1) * HALF
                ]
    for half in range(2):
        o_ref[:, :, half * HALF : (half + 1) * HALF] = rows[half].reshape(GROUP, GROUP, HALF)


def finish(perm, w):
    return pl.pallas_call(
        finish_kernel,
        grid=(4,),
        out_shape=jax.ShapeDtypeStruct((BLOCK, GROUP, NR), f32),
        in_specs=[
            pl.BlockSpec((NR, NR), lambda n: (0, 0)),
            pl.BlockSpec((2, GROUP, GROUP, HALF), lambda n: (0, 0, n, 0)),
        ],
        out_specs=pl.BlockSpec((GROUP, GROUP, NR), lambda n: (n, 0, 0)),
        scratch_shapes=[pltpu.VMEM((2, GROUP * GROUP, HALF), f32)],
        compiler_params=pltpu.CompilerParams(vmem_limit_bytes=16 << 20),
        name="finish",
    )(perm, w)


def body(tables, charge, outer_held, end_held):
    forward, backward, *hartleys = (jnp.asarray(t) for t in tables)
    outer = outer_held.reshape(1, NZ)
    end = end_held.reshape(1, NR)
    w, scales = run(charge, outer, end, (forward, *hartleys))
    potential = finish(backward, w.reshape(2, GROUP, BLOCK, HALF))
    return (potential, scales)


def solution(mesh):
    in_specs = (P("phi", "gz", None), P(), P())
    out_specs = (P("phi", "gz", None), P(None, "phi"))
    perm = parity_table()
    tables = (perm, np.ascontiguousarray(perm.T), *hartley_tables())
    return jax.shard_map(
        functools.partial(body, tables), mesh=mesh, in_specs=in_specs, out_specs=out_specs, check_vma=False
    )
```

```python
import functools
import math

import jax
import jax.numpy as jnp
import numpy as np
from jax import lax
from jax.experimental import pallas as pl
from jax.experimental.pallas import tpu as pltpu
from jax.sharding import PartitionSpec as P

NPHI = 1024
VCYC = 2
NU = 2
KC = 3
RIN = 131
NR = 256
NZ = 256
HALF = 128
FEW = 4
GROUP = 16
BLOCK = 64
MESH = pl.DeviceIdType.MESH

relaxation = 0.8
small_floor = 1e-06
f32 = jnp.float32
bf16 = jnp.bfloat16

PAD = 8
CH = 32


def hartley_tables():
    k = np.arange(NPHI)
    phase = (np.outer(k, k) % NPHI) * (2.0 * math.pi / NPHI)
    table = ((np.cos(phase) + np.sin(phase)) / math.sqrt(NPHI)).astype(np.float32)
    order = k.reshape(GROUP, GROUP, FEW).transpose(1, 0, 2).reshape(-1)
    table = table[order]
    high = table.astype(jnp.bfloat16)
    low = (table - high.astype(np.float32)).astype(jnp.bfloat16)
    return high, low, np.ascontiguousarray(high.T), np.ascontiguousarray(low.T)


def parity_table():
    perm = np.zeros((NR, NR), np.float32)
    i = np.arange(NR)
    perm[i, (i % 2) * HALF + i // 2] = 1.0
    return perm.astype(jnp.bfloat16)


def split(values):
    high = values.astype(bf16)
    low = (values - high.astype(f32)).astype(bf16)
    return high, low


def lane_ids(rows=1):
    return lax.broadcasted_iota(jnp.int32, (rows, HALF), 1)


def fine_rows(parity):
    i = 2 * lane_ids() + parity
    radius = i.astype(f32) + (RIN + 0.5)
    inward = (radius - 0.5) / radius
    outward = (radius + 0.5) / radius
    return radius, inward, outward


def coarse_rows():
    radius = 2.0 * lane_ids().astype(f32) + (RIN + 1.0)
    inward = (radius - 1.0) / (4.0 * radius)
    outward = (radius + 1.0) / (4.0 * radius)
    return radius, inward, outward


def as_column(row):
    square = jnp.broadcast_to(row, (HALF, HALF))
    diag = lax.broadcasted_iota(jnp.int32, (HALF, HALF), 0) == lane_ids(HALF)
    return jnp.sum(jnp.where(diag, square, 0.0), axis=1, keepdims=True)


def setup_base(base_ref, outer_rows, end_rows):
    y = lax.broadcasted_iota(jnp.int32, (HALF, HALF), 0)
    j = lane_ids(HALF)
    for zp in range(2):
        open_outer = 1.0 - as_column(outer_rows[zp])
        for ip in range(2):
            _, inward, outward = fine_rows(ip)
            open_end = 1.0 - end_rows[ip]
            value = jnp.broadcast_to(inward + outward + 2.0, (HALF, HALF))
            if ip == 1:
                value = value - jnp.where(j == HALF - 1, outward * open_outer, 0.0)
            edge = 0 if zp == 0 else HALF - 1
            value = value - jnp.where(y == edge, open_end, 0.0)
            base_ref[2 * zp + ip] = value
    _, inward, outward = coarse_rows()
    open_outer = 1.0 - as_column(outer_rows[0])
    open_end = 1.0 - end_rows[0]
    value = jnp.broadcast_to(inward + outward + 0.5, (HALF, HALF))
    value = value - jnp.where(j == HALF - 1, outward * open_outer, 0.0)
    value = value - jnp.where((y == 0) | (y == HALF - 1), 0.25 * open_end, 0.0)
    base_ref[4] = value


def left_of(value):
    return pltpu.roll(value, 1, 1)


def right_of(value):
    return pltpu.roll(value, HALF - 1, 1)


def solve_mode(mode, f_ref, base_ref, d_ref, w_ref, va, vb, r_ref, ca, cb, cr_ref, write):
    order = jnp.minimum(mode, NPHI - mode).astype(f32)
    square = order * order
    rows_e = fine_rows(0)
    rows_o = fine_rows(1)
    first = lane_ids() == 0
    last = lane_ids() == HALF - 1
    in_e = jnp.where(first, 0.0, rows_e[1])
    out_e = rows_e[2]
    in_o = rows_o[1]
    out_o = jnp.where(last, 0.0, rows_o[2])
    radius_c, in_c0, out_c0 = coarse_rows()
    in_c = jnp.where(first, 0.0, in_c0)
    out_c = jnp.where(last, 0.0, out_c0)
    term_e = square / (rows_e[0] * rows_e[0])
    term_o = square / (rows_o[0] * rows_o[0])
    term_c = square / (radius_c * radius_c)
    chunks = [pl.ds(s, CH) for s in range(0, HALF, CH)]
    padded = [pl.ds(PAD + s, CH) for s in range(0, HALF, CH)]
    above = [pl.ds(PAD + s - 1, CH) for s in range(0, HALF, CH)]
    below = [pl.ds(PAD + s + 1, CH) for s in range(0, HALF, CH)]
    count = len(chunks)

    def neighbours(v, c):
        ee, eo, oe, oo = (v[q, padded[c], :] for q in range(4))
        oe_up, oo_up = v[2, above[c], :], v[3, above[c], :]
        ee_dn, eo_dn = v[0, below[c], :], v[1, below[c], :]
        n_ee = (oe_up + oe) + (in_e * left_of(eo) + out_e * eo)
        n_eo = (oo_up + oo) + (in_o * ee + out_o * right_of(ee))
        n_oe = (ee + ee_dn) + (in_e * left_of(oo) + out_e * oo)
        n_oo = (eo + eo_dn) + (in_o * oe + out_o * right_of(oe))
        return (ee, eo, oe, oo), (n_ee, n_eo, n_oe, n_oo)

    def sweep(src, dst, emit=None):
        for c in range(count):
            centre, near = neighbours(src, c)
            for q in range(4):
                value = (1.0 - relaxation) * centre[q] + w_ref[q, chunks[c], :] * (
                    f_ref[q, chunks[c], :] + near[q]
                )
                if emit is None:
                    dst[q, padded[c], :] = value
                else:
                    emit(q, c * CH, value)

    for c in range(count):
        for q in range(4):
            d = base_ref[q, chunks[c], :] + (term_e if q % 2 == 0 else term_o)
            w = relaxation / d
            d_ref[q, chunks[c], :] = d
            w_ref[q, chunks[c], :] = w
            va[q, padded[c], :] = w * f_ref[q, chunks[c], :]
        d_ref[4, chunks[c], :] = relaxation / (base_ref[4, chunks[c], :] + term_c)

    factors = []
    cur, other = va, vb
    for cycle in range(VCYC):
        for s in range(1 if cycle == 0 else 0, NU):
            sweep(cur, other)
            cur, other = other, cur
        for c in range(count):
            centre, near = neighbours(cur, c)
            total = None
            for q in range(4):
                res = f_ref[q, chunks[c], :] + near[q] - d_ref[q, chunks[c], :] * centre[q]
                r_ref[q, chunks[c], :] = res
                total = res if total is None else total + res
            total = total * 0.25
            cr_ref[chunks[c], :] = total
            ca[padded[c], :] = d_ref[4, chunks[c], :] * total
        now, later = ca, cb
        for s in range(KC):
            for c in range(count):
                w = now[padded[c], :]
                near = (
                    in_c * left_of(w)
                    + out_c * right_of(w)
                    + 0.25 * (now[above[c], :] + now[below[c], :])
                )
                later[padded[c], :] = (1.0 - relaxation) * w + d_ref[4, chunks[c], :] * (
                    cr_ref[chunks[c], :] + near
                )
            now, later = later, now
        top = jnp.zeros((8, HALF), f32)
        bottom = jnp.zeros((8, HALF), f32)
        for c in range(count):
            w = now[padded[c], :]
            low_e = in_e * left_of(w) + out_e * w
            low_o = in_o * w + out_o * right_of(w)
            up = now[above[c], :] + w
            down = now[below[c], :] + w
            for q in range(4):
                image = d_ref[q, chunks[c], :] * w - (low_e if q % 2 == 0 else low_o)
                image = image - (up if q < 2 else down)
                res = r_ref[q, chunks[c], :]
                for g in range(CH // 8):
                    part = image[8 * g : 8 * g + 8]
                    top = top + res[8 * g : 8 * g + 8] * part
                    bottom = bottom + part * part
        factor = jnp.sum(top, keepdims=True) / (jnp.sum(bottom, keepdims=True) + small_floor)
        factors.append(factor)
        for c in range(count):
            add = factor * now[padded[c], :]
            for q in range(4):
                cur[q, padded[c], :] = cur[q, padded[c], :] + add
        for s in range(NU):
            if cycle == VCYC - 1 and s == NU - 1:
                sweep(cur, None, write)
            else:
                sweep(cur, other)
                cur, other = other, cur
    return factors


def block(index):
    return pl.ds(pl.multiple_of(index * BLOCK, BLOCK), BLOCK)


def peers(me, action):
    def step(o, carry):
        action(lax.rem(me + o, GROUP))
        return carry

    lax.fori_loop(1, GROUP, step, 0)


class Exchange:
    def __init__(self, axis, src, dst, send, recv):
        self.axis, self.src, self.dst, self.send, self.recv = axis, src, dst, send, recv
        self.me = lax.axis_index(axis)

    def copy(self, par, source, target, t, sem):
        return pltpu.make_async_remote_copy(
            src_ref=self.src.at[par, source],
            dst_ref=self.dst.at[par, target],
            send_sem=self.send.at[par],
            recv_sem=self.recv.at[sem],
            device_id={self.axis: t},
            device_id_type=MESH,
        )

    def start(self, par, t):
        self.copy(par, block(t), block(self.me), t, par).start()

    def start_all(self, par):
        peers(self.me, lambda t: self.start(par, t))

    def start_mode(self, par, m, sem):
        rows = lambda n: pl.ds(pl.multiple_of(n * BLOCK + m * GROUP, GROUP), GROUP)
        peers(self.me, lambda t: self.copy(par, rows(t), rows(self.me), t, sem).start())

    def keep(self, par):
        self.dst[par, block(self.me), :] = self.src[par, block(self.me), :]

    def whole(self, par, rows, sem):
        t = lax.rem(self.me + 1, GROUP)
        return self.copy(par, pl.ds(0, rows), pl.ds(0, rows), t, sem)

    def wait_recv(self, par):
        self.whole(par, (GROUP - 1) * BLOCK, par).wait_recv()

    def wait_recv_mode(self, par, sem):
        self.whole(par, (GROUP - 1) * GROUP, sem).wait_recv()

    def wait_send(self, par):
        self.whole(par, (GROUP - 1) * BLOCK, par).wait_send()


def hartley(high, low, src, par, xs, exchange):
    for piece in range(4):
        rows = pl.ds(piece * 256, 256)
        h, l = split(src[par, rows, :])
        xs[rows, :HALF] = h
        xs[rows, HALF:] = l
    me = exchange.me

    def step(n, carry):
        piece = lax.rem(me // 4 + n, 4)
        rows = pl.ds(pl.multiple_of(piece * 256, 256), 256)
        both = jnp.dot(high[rows, :], xs[...], preferred_element_type=f32)
        rest = jnp.dot(low[rows, :], xs[:, :HALF], preferred_element_type=f32)
        exchange.src[par, rows, :] = both[:, :HALF] + (both[:, HALF:] + rest)
        for j in range(4):
            t = piece * 4 + lax.rem(me + j, 4)

            @pl.when(t != me)
            def _():
                exchange.start(par, t)

        return carry

    lax.fori_loop(0, 4, step, 0)


def main_kernel(
    charge_ref, outer_ref, end_ref, perm_ref, fh_ref, fl_ref, bh_ref, bl_ref,
    w_ref, s_ref,
    xin, xp, t1, r1, s1, r2, r3, r4, o4, p3, p2, q1, v1, xs,
    fh, fl, bh, bl,
    f, base, d, w, va, vb, r, ca, cb, cr, sc_src, sc,
    in_sem, table_sem, keep_sem, send, recv, sc_send, sc_recv,
):
    phi, gz = lax.axis_index("phi"), lax.axis_index("gz")
    load = pltpu.make_async_copy(charge_ref, xin, in_sem)
    load.start()
    tables = [
        pltpu.make_async_copy(src, dst, table_sem.at[n])
        for n, (src, dst) in enumerate(((fh_ref, fh), (fl_ref, fl), (bh_ref, bh), (bl_ref, bl)))
    ]
    for copy in tables:
        copy.start()
    barrier = pltpu.get_barrier_semaphore()
    for axis, me in (("phi", phi), ("gz", gz)):
        peers(
            me,
            lambda t: pl.semaphore_signal(barrier, inc=1, device_id={axis: t}, device_id_type=MESH),
        )

    first = Exchange("phi", t1, r1, send.at[0], recv.at[0])
    second = Exchange("gz", s1, r2, send.at[1], recv.at[1])
    third = Exchange("phi", r3, r4, send.at[2], recv.at[2])
    fourth = Exchange("phi", o4, p3, send.at[3], recv.at[3])
    fifth = Exchange("gz", p2, q1, send.at[4], recv.at[4])
    sixth = Exchange("phi", v1, w_ref, send.at[5], recv.at[5])

    load.wait()
    for piece in range(4):
        rows = pl.ds(piece * 256, 256)
        h, l = split(xin[piece * 16 : (piece + 1) * 16].reshape(256, NR))
        value = jnp.dot(h, perm_ref[...], preferred_element_type=f32) + jnp.dot(
            l, perm_ref[...], preferred_element_type=f32
        )
        xp[0, rows, :] = value[:, :HALF]
        xp[1, rows, :] = value[:, HALF:]
    for par in range(2):
        for z in range(GROUP):
            t1[par, z * BLOCK : (z + 1) * BLOCK, :] = xp[par, pl.ds(z, BLOCK, stride=GROUP), :]
    pl.semaphore_wait(barrier, 2 * (GROUP - 1))

    first.start_all(0)
    first.start_all(1)
    first.keep(0)
    first.keep(1)

    held = jnp.concatenate([outer_ref[...], end_ref[...]], axis=0).astype(f32).astype(bf16)
    held = jnp.concatenate([held] * 8, axis=0)
    held = jnp.dot(held, perm_ref[...], preferred_element_type=f32)
    setup_base(base, [held[0:1, :HALF], held[0:1, HALF:]], [held[1:2, :HALF], held[1:2, HALF:]])
    for ref in (va, vb):
        ref[:, 0:PAD, :] = jnp.zeros((4, PAD, HALF), f32)
        ref[:, HALF + PAD :, :] = jnp.zeros((4, PAD, HALF), f32)
    for ref in (ca, cb):
        ref[0:PAD, :] = jnp.zeros((PAD, HALF), f32)
        ref[HALF + PAD :, :] = jnp.zeros((PAD, HALF), f32)
    sc_src[...] = jnp.zeros((8, HALF), f32)
    for copy in tables:
        copy.wait()

    for par in range(2):
        first.wait_recv(par)
        hartley(fh, fl, r1, par, xs, second)
        second.keep(par)
        second.wait_recv(par)
        for b in range(GROUP):
            r3[par, pl.ds(b, BLOCK, stride=GROUP), :] = r2[par, b * BLOCK : (b + 1) * BLOCK, :]
        if par == 0:
            third.start_all(par)
        else:
            for m in range(FEW):
                third.start_mode(par, m, 1 + m)
        third.keep(par)

    third.wait_recv(0)

    def solve_step(m, carry):
        third.wait_recv_mode(1, 1 + m)
        mode = (phi * GROUP + gz) * FEW + m
        for q in range(4):
            for b in range(GROUP):
                f[q, 8 * b : 8 * b + 8, :] = r4[
                    q % 2, pl.ds((q // 2) * BLOCK + m * GROUP + b, 8, stride=HALF), :
                ]

        def write(q, start, value):
            for g in range(CH // 8):
                b = start // 8 + g
                o4[q % 2, pl.ds((q // 2) * BLOCK + m * GROUP + b, 8, stride=HALF), :] = value[
                    8 * g : 8 * g + 8
                ]

        factors = solve_mode(mode, f, base, d, w, va, vb, r, ca, cb, cr, write)
        row_ids = lax.broadcasted_iota(jnp.int32, (8, HALF), 0)
        lanes = lane_ids(8)
        for cycle in range(VCYC):
            here = (row_ids == cycle) & (lanes == gz * FEW + m)
            sc_src[...] = sc_src[...] + jnp.where(here, factors[cycle], 0.0)
        fourth.start_mode(0, m, 0)
        return carry

    lax.fori_loop(0, FEW, solve_step, 0)

    fourth.start_all(1)
    fourth.keep(0)
    fourth.keep(1)

    def scale_copy(source, target, t):
        return pltpu.make_async_remote_copy(
            src_ref=source,
            dst_ref=target,
            send_sem=sc_send,
            recv_sem=sc_recv,
            device_id={"gz": t},
            device_id_type=MESH,
        )

    peers(gz, lambda t: scale_copy(sc_src, sc.at[gz], t).start())
    sc[gz] = sc_src[...]

    for par in range(2):
        fourth.wait_recv(par)
        for b in range(GROUP):
            p2[par, b * BLOCK : (b + 1) * BLOCK, :] = p3[par, pl.ds(b, BLOCK, stride=GROUP), :]
        fifth.start_all(par)
        fifth.keep(par)
        fifth.wait_recv(par)
        hartley(bh, bl, q1, par, xs, sixth)
        pltpu.make_async_copy(
            v1.at[par, block(phi)], w_ref.at[par, block(phi)], keep_sem.at[par]
        ).start()

    others = sc.at[pl.ds(0, GROUP - 1)]
    all_scales = scale_copy(others, others, lax.rem(gz + 1, GROUP))
    all_scales.wait_recv()
    total = sc[0]
    for n in range(1, GROUP):
        total = total + sc[n]
    s_ref[...] = total[:VCYC, :BLOCK]

    for exchange in (first, second, third, fourth, fifth):
        for par in range(2):
            exchange.wait_send(par)
    all_scales.wait_send()
    for par in range(2):
        sixth.wait_recv(par)
        sixth.wait_send(par)
        pltpu.make_async_copy(
            v1.at[par, block(phi)], w_ref.at[par, block(phi)], keep_sem.at[par]
        ).wait()


def run(charge, outer, end, tables):
    rows = lambda: pltpu.VMEM((2, NPHI, HALF), f32)
    quad = lambda n: pltpu.VMEM((n, HALF, HALF), f32)
    table = lambda: pltpu.VMEM((NPHI, NPHI), bf16)
    whole = pl.BlockSpec(memory_space=pltpu.VMEM)
    away = pl.BlockSpec(memory_space=pl.ANY)
    return pl.pallas_call(
        main_kernel,
        out_shape=(
            jax.ShapeDtypeStruct((2, NPHI, HALF), f32),
            jax.ShapeDtypeStruct((VCYC, BLOCK), f32),
        ),
        in_specs=[away, whole, whole, whole, away, away, away, away],
        out_specs=(away, whole),
        scratch_shapes=[
            pltpu.VMEM((BLOCK, GROUP, NR), f32),
            *[rows() for _ in range(12)],
            pltpu.VMEM((NPHI, NR), bf16),
            table(), table(), table(), table(),
            quad(4), quad(5), quad(5), quad(4),
            pltpu.VMEM((4, HALF + 2 * PAD, HALF), f32),
            pltpu.VMEM((4, HALF + 2 * PAD, HALF), f32),
            quad(4),
            pltpu.VMEM((HALF + 2 * PAD, HALF), f32),
            pltpu.VMEM((HALF + 2 * PAD, HALF), f32),
            pltpu.VMEM((HALF, HALF), f32),
            pltpu.VMEM((8, HALF), f32),
            pltpu.VMEM((GROUP, 8, HALF), f32),
            pltpu.SemaphoreType.DMA,
            pltpu.SemaphoreType.DMA((4,)),
            pltpu.SemaphoreType.DMA((2,)),
            pltpu.SemaphoreType.DMA((6, 2)),
            pltpu.SemaphoreType.DMA((6, 5)),
            pltpu.SemaphoreType.DMA,
            pltpu.SemaphoreType.DMA,
        ],
        compiler_params=pltpu.CompilerParams(
            collective_id=0, has_side_effects=True, vmem_limit_bytes=62 << 20
        ),
        name="modes",
    )(charge, outer, end, *tables)


def finish_kernel(perm_ref, w_ref, o_ref, rows):
    for z in range(0, GROUP, 4):
        flat = jnp.concatenate(
            [w_ref[0, z : z + 4].reshape(4 * GROUP, HALF), w_ref[1, z : z + 4].reshape(4 * GROUP, HALF)],
            axis=1,
        )
        h, l = split(flat)
        value = jnp.dot(h, perm_ref[...], preferred_element_type=f32) + jnp.dot(
            l, perm_ref[...], preferred_element_type=f32
        )
        for g in range(4):
            for half in range(2):
                rows[half, pl.ds(z + g, GROUP, stride=GROUP), :] = value[
                    g * GROUP : (g + 1) * GROUP, half * HALF : (half + 1) * HALF
                ]
    for half in range(2):
        o_ref[:, :, half * HALF : (half + 1) * HALF] = rows[half].reshape(GROUP, GROUP, HALF)


def finish(perm, w):
    return pl.pallas_call(
        finish_kernel,
        grid=(4,),
        out_shape=jax.ShapeDtypeStruct((BLOCK, GROUP, NR), f32),
        in_specs=[
            pl.BlockSpec((NR, NR), lambda n: (0, 0)),
            pl.BlockSpec((2, GROUP, GROUP, HALF), lambda n: (0, 0, n, 0)),
        ],
        out_specs=pl.BlockSpec((GROUP, GROUP, NR), lambda n: (n, 0, 0)),
        scratch_shapes=[pltpu.VMEM((2, GROUP * GROUP, HALF), f32)],
        compiler_params=pltpu.CompilerParams(vmem_limit_bytes=16 << 20),
        name="finish",
    )(perm, w)


def body(tables, charge, outer_held, end_held):
    forward, backward, *hartleys = (jnp.asarray(t) for t in tables)
    outer = outer_held.reshape(1, NZ)
    end = end_held.reshape(1, NR)
    w, scales = run(charge, outer, end, (forward, *hartleys))
    potential = finish(backward, w.reshape(2, GROUP, BLOCK, HALF))
    return (potential, scales)


def solution(mesh):
    in_specs = (P("phi", "gz", None), P(), P())
    out_specs = (P("phi", "gz", None), P(None, "phi"))
    perm = parity_table()
    tables = (perm, np.ascontiguousarray(perm.T), *hartley_tables())
    return jax.shard_map(
        functools.partial(body, tables), mesh=mesh, in_specs=in_specs, out_specs=out_specs, check_vma=False
    )
```

```python
import functools
import math

import jax
import jax.numpy as jnp
import numpy as np
from jax import lax
from jax.experimental import pallas as pl
from jax.experimental.pallas import tpu as pltpu
from jax.sharding import PartitionSpec as P

NPHI = 1024
VCYC = 2
NU = 2
KC = 3
RIN = 131
NR = 256
NZ = 256
HALF = 128
FEW = 4
GROUP = 16
BLOCK = 64
MESH = pl.DeviceIdType.MESH

relaxation = 0.8
small_floor = 1e-06
f32 = jnp.float32
bf16 = jnp.bfloat16

PAD = 8
CH = 32


def hartley_tables():
    k = np.arange(NPHI)
    phase = (np.outer(k, k) % NPHI) * (2.0 * math.pi / NPHI)
    table = ((np.cos(phase) + np.sin(phase)) / math.sqrt(NPHI)).astype(np.float32)
    order = k.reshape(GROUP, GROUP, FEW).transpose(1, 2, 0).reshape(-1)
    table = table[order]
    high = table.astype(jnp.bfloat16)
    low = (table - high.astype(np.float32)).astype(jnp.bfloat16)
    return high, low, np.ascontiguousarray(high.T), np.ascontiguousarray(low.T)


def split(values):
    high = values.astype(bf16)
    low = (values - high.astype(f32)).astype(bf16)
    return high, low


def lane_ids(rows=1):
    return lax.broadcasted_iota(jnp.int32, (rows, HALF), 1)


def fine_rows(parity):
    i = 2 * lane_ids() + parity
    radius = i.astype(f32) + (RIN + 0.5)
    inward = (radius - 0.5) / radius
    outward = (radius + 0.5) / radius
    return radius, inward, outward


def coarse_rows():
    radius = 2.0 * lane_ids().astype(f32) + (RIN + 1.0)
    inward = (radius - 1.0) / (4.0 * radius)
    outward = (radius + 1.0) / (4.0 * radius)
    return radius, inward, outward


def as_column(row):
    square = jnp.broadcast_to(row, (HALF, HALF))
    diag = lax.broadcasted_iota(jnp.int32, (HALF, HALF), 0) == lane_ids(HALF)
    return jnp.sum(jnp.where(diag, square, 0.0), axis=1, keepdims=True)


def setup_base(base_ref, outer_rows, end_rows):
    y = lax.broadcasted_iota(jnp.int32, (HALF, HALF), 0)
    j = lane_ids(HALF)
    for zp in range(2):
        open_outer = 1.0 - as_column(outer_rows[zp])
        for ip in range(2):
            _, inward, outward = fine_rows(ip)
            open_end = 1.0 - end_rows[ip]
            value = jnp.broadcast_to(inward + outward + 2.0, (HALF, HALF))
            if ip == 1:
                value = value - jnp.where(j == HALF - 1, outward * open_outer, 0.0)
            edge = 0 if zp == 0 else HALF - 1
            value = value - jnp.where(y == edge, open_end, 0.0)
            base_ref[2 * zp + ip] = value
    _, inward, outward = coarse_rows()
    open_outer = 1.0 - as_column(outer_rows[0])
    open_end = 1.0 - end_rows[0]
    value = jnp.broadcast_to(inward + outward + 0.5, (HALF, HALF))
    value = value - jnp.where(j == HALF - 1, outward * open_outer, 0.0)
    value = value - jnp.where((y == 0) | (y == HALF - 1), 0.25 * open_end, 0.0)
    base_ref[4] = value


def parity_matrix(half):
    cell = lax.broadcasted_iota(jnp.int32, (HALF, HALF), 0)
    lane = lax.broadcasted_iota(jnp.int32, (HALF, HALF), 1)
    second = (cell % 2) != half
    target = cell // 2 + jnp.where(second, HALF // 2, 0)
    return jnp.where(lane == target, 1.0, 0.0)


def even_odd(first, second):
    low = lane_ids(first.shape[0]) < HALF // 2
    even = jnp.where(low, first, second)
    odd = pltpu.roll(jnp.where(low, second, first), HALF // 2, 1)
    return even, odd


def two_halves(even, odd):
    low = lane_ids(even.shape[0]) < HALF // 2
    odd = pltpu.roll(odd, HALF // 2, 1)
    return jnp.where(low, even, odd), jnp.where(low, odd, even)


def left_of(value):
    return pltpu.roll(value, 1, 1)


def right_of(value):
    return pltpu.roll(value, HALF - 1, 1)


def solve_mode(mode, f_ref, base_ref, d_ref, w_ref, va, vb, r_ref, ca, cb, cr_ref, write):
    order = jnp.minimum(mode, NPHI - mode).astype(f32)
    square = order * order
    rows_e = fine_rows(0)
    rows_o = fine_rows(1)
    first = lane_ids() == 0
    last = lane_ids() == HALF - 1
    in_e = jnp.where(first, 0.0, rows_e[1])
    out_e = rows_e[2]
    in_o = rows_o[1]
    out_o = jnp.where(last, 0.0, rows_o[2])
    radius_c, in_c0, out_c0 = coarse_rows()
    in_c = jnp.where(first, 0.0, in_c0)
    out_c = jnp.where(last, 0.0, out_c0)
    term_e = square / (rows_e[0] * rows_e[0])
    term_o = square / (rows_o[0] * rows_o[0])
    term_c = square / (radius_c * radius_c)
    chunks = [pl.ds(s, CH) for s in range(0, HALF, CH)]
    padded = [pl.ds(PAD + s, CH) for s in range(0, HALF, CH)]
    above = [pl.ds(PAD + s - 1, CH) for s in range(0, HALF, CH)]
    below = [pl.ds(PAD + s + 1, CH) for s in range(0, HALF, CH)]
    count = len(chunks)

    def neighbours(v, c):
        ee, eo, oe, oo = (v[q, padded[c], :] for q in range(4))
        oe_up, oo_up = v[2, above[c], :], v[3, above[c], :]
        ee_dn, eo_dn = v[0, below[c], :], v[1, below[c], :]
        n_ee = (oe_up + oe) + (in_e * left_of(eo) + out_e * eo)
        n_eo = (oo_up + oo) + (in_o * ee + out_o * right_of(ee))
        n_oe = (ee + ee_dn) + (in_e * left_of(oo) + out_e * oo)
        n_oo = (eo + eo_dn) + (in_o * oe + out_o * right_of(oe))
        return (ee, eo, oe, oo), (n_ee, n_eo, n_oe, n_oo)

    def sweep(src, dst, emit=None):
        for c in range(count):
            centre, near = neighbours(src, c)
            values = []
            for q in range(4):
                value = (1.0 - relaxation) * centre[q] + w_ref[q, chunks[c], :] * (
                    f_ref[q, chunks[c], :] + near[q]
                )
                if emit is None:
                    dst[q, padded[c], :] = value
                values.append(value)
            if emit is not None:
                emit(c * CH, values)

    for c in range(count):
        for q in range(4):
            d = base_ref[q, chunks[c], :] + (term_e if q % 2 == 0 else term_o)
            w = relaxation / d
            d_ref[q, chunks[c], :] = d
            w_ref[q, chunks[c], :] = w
            va[q, padded[c], :] = w * f_ref[q, chunks[c], :]
        d_ref[4, chunks[c], :] = relaxation / (base_ref[4, chunks[c], :] + term_c)

    factors = []
    cur, other = va, vb
    for cycle in range(VCYC):
        for s in range(1 if cycle == 0 else 0, NU):
            sweep(cur, other)
            cur, other = other, cur
        for c in range(count):
            centre, near = neighbours(cur, c)
            total = None
            for q in range(4):
                res = f_ref[q, chunks[c], :] + near[q] - d_ref[q, chunks[c], :] * centre[q]
                r_ref[q, chunks[c], :] = res
                total = res if total is None else total + res
            total = total * 0.25
            cr_ref[chunks[c], :] = total
            ca[padded[c], :] = d_ref[4, chunks[c], :] * total
        now, later = ca, cb
        for s in range(KC):
            for c in range(count):
                w = now[padded[c], :]
                near = (
                    in_c * left_of(w)
                    + out_c * right_of(w)
                    + 0.25 * (now[above[c], :] + now[below[c], :])
                )
                later[padded[c], :] = (1.0 - relaxation) * w + d_ref[4, chunks[c], :] * (
                    cr_ref[chunks[c], :] + near
                )
            now, later = later, now
        top = jnp.zeros((8, HALF), f32)
        bottom = jnp.zeros((8, HALF), f32)
        for c in range(count):
            w = now[padded[c], :]
            low_e = in_e * left_of(w) + out_e * w
            low_o = in_o * w + out_o * right_of(w)
            up = now[above[c], :] + w
            down = now[below[c], :] + w
            for q in range(4):
                image = d_ref[q, chunks[c], :] * w - (low_e if q % 2 == 0 else low_o)
                image = image - (up if q < 2 else down)
                res = r_ref[q, chunks[c], :]
                for g in range(CH // 8):
                    part = image[8 * g : 8 * g + 8]
                    top = top + res[8 * g : 8 * g + 8] * part
                    bottom = bottom + part * part
        factor = jnp.sum(top, keepdims=True) / (jnp.sum(bottom, keepdims=True) + small_floor)
        factors.append(factor)
        for c in range(count):
            add = factor * now[padded[c], :]
            for q in range(4):
                cur[q, padded[c], :] = cur[q, padded[c], :] + add
        for s in range(NU):
            if cycle == VCYC - 1 and s == NU - 1:
                sweep(cur, None, write)
            else:
                sweep(cur, other)
                cur, other = other, cur
    return factors


def block(index):
    return pl.ds(pl.multiple_of(index * BLOCK, BLOCK), BLOCK)


def peers(me, action):
    def step(n, carry):
        away = (n // 2 + 1) * (1 - 2 * lax.rem(n, 2))
        action(lax.rem(me + GROUP + away, GROUP))
        return carry

    lax.fori_loop(0, GROUP - 1, step, 0)


class Exchange:
    def __init__(self, axis, src, dst, send, recv, base):
        self.axis, self.src, self.dst, self.send, self.recv = axis, src, dst, send, recv
        self.base = base
        self.me = lax.axis_index(axis)

    def copy(self, par, source, target, t, sem):
        return pltpu.make_async_remote_copy(
            src_ref=self.src.at[par, source],
            dst_ref=self.dst.at[par, target],
            send_sem=self.send.at[par],
            recv_sem=self.recv.at[self.base + sem],
            device_id={self.axis: t},
            device_id_type=MESH,
        )

    def start(self, par, t):
        self.copy(par, block(t), block(self.me), t, par).start()

    def start_all(self, par):
        peers(self.me, lambda t: self.start(par, t))

    def start_mode(self, par, m, sem):
        rows = lambda n: pl.ds(pl.multiple_of(n * BLOCK + m * GROUP, GROUP), GROUP)
        peers(self.me, lambda t: self.copy(par, rows(t), rows(self.me), t, sem).start())

    def keep(self, par):
        self.dst[par, block(self.me), :] = self.src[par, block(self.me), :]

    def whole(self, par, rows, sem):
        t = lax.rem(self.me + 1, GROUP)
        return self.copy(par, pl.ds(0, rows), pl.ds(0, rows), t, sem)

    def wait_recv(self, par):
        self.whole(par, (GROUP - 1) * BLOCK, par).wait_recv()

    def wait_recv_mode(self, par, sem):
        self.whole(par, (GROUP - 1) * GROUP, sem).wait_recv()

    def wait_send(self, par):
        self.whole(par, (GROUP - 1) * BLOCK, par).wait_send()


def hartley(high, low, src, par, order, xs, exchange):
    for piece in range(4):
        rows = pl.ds(piece * 256, 256)
        h, l = split(src[par, rows, :])
        xs[rows, :HALF] = jnp.dot(h, order, preferred_element_type=f32).astype(bf16)
        xs[rows, HALF:] = jnp.dot(l, order, preferred_element_type=f32).astype(bf16)
    me = exchange.me

    def step(n, carry):
        piece = lax.rem(me // 4 + n, 4)
        rows = pl.ds(pl.multiple_of(piece * 256, 256), 256)
        both = jnp.dot(high[rows, :], xs[...], preferred_element_type=f32)
        rest = jnp.dot(low[rows, :], xs[:, :HALF], preferred_element_type=f32)
        exchange.src[par, rows, :] = both[:, :HALF] + (both[:, HALF:] + rest)
        for j in range(4):
            t = piece * 4 + lax.rem(me + j, 4)

            @pl.when(t != me)
            def _():
                exchange.start(par, t)

        return carry

    lax.fori_loop(0, 4, step, 0)


def main_kernel(
    charge_ref, outer_ref, end_ref, fh_ref, fl_ref, bh_ref, bl_ref,
    w_ref, s_ref,
    outer, end, xin, t1, r1, s1, r2, r3, r4, o4, p3, p2, q1, v1, order, xs,
    fh, fl, bh, bl,
    f, base, d, w, va, vb, r, ca, cb, cr, sc_src, sc,
    in_sem, table_sem, send, recv, sc_send, sc_recv,
):
    phi, gz = lax.axis_index("phi"), lax.axis_index("gz")
    loads = [
        pltpu.make_async_copy(charge_ref.at[:, pl.ds(half * HALF, HALF)], xin.at[half], in_sem.at[half])
        for half in range(2)
    ]
    for copy in loads:
        copy.start()
    tables = [
        pltpu.make_async_copy(src, dst, table_sem.at[n])
        for n, (src, dst) in enumerate(((outer_ref, outer), (end_ref, end), (fh_ref, fh), (fl_ref, fl), (bh_ref, bh), (bl_ref, bl)))
    ]
    for copy in tables:
        copy.start()
    barrier = pltpu.get_barrier_semaphore()
    for axis, me in (("phi", phi), ("gz", gz)):
        peers(
            me,
            lambda t: pl.semaphore_signal(barrier, inc=1, device_id={axis: t}, device_id_type=MESH),
        )

    first = Exchange("phi", t1, r1, send.at[0], recv, 0)
    second = Exchange("gz", s1, r2, send.at[1], recv, 2)
    third = Exchange("phi", r3, r4, send.at[2], recv, 4)
    fourth = Exchange("phi", o4, p3, send.at[3], recv, 9)
    fifth = Exchange("gz", p2, q1, send.at[4], recv, 17)
    sixth = Exchange("phi", v1, w_ref, send.at[5], recv, 19)

    for half in range(2):
        loads[half].wait()
        if half == 0:
            pl.semaphore_wait(barrier, 2 * (GROUP - 1))

        def regroup(t):
            t1[half, block(t), :] = xin[half, pl.ds(t, BLOCK, stride=GROUP), :]
            first.start(half, t)

        peers(phi, regroup)
        r1[half, block(phi), :] = xin[half, pl.ds(phi, BLOCK, stride=GROUP), :]

    for copy in tables:
        copy.wait()
    orders = [parity_matrix(0), parity_matrix(1)]
    held = jnp.concatenate([outer[...]] * 4 + [end[...]] * 4, axis=0).astype(f32)
    held = even_odd(*(
        jnp.dot(
            held[:, n * HALF : (n + 1) * HALF].astype(bf16),
            orders[n].astype(bf16),
            preferred_element_type=f32,
        )
        for n in range(2)
    ))
    setup_base(base, [row[0:1] for row in held], [row[4:5] for row in held])
    for n in range(2):
        order[n] = orders[n].astype(bf16)
        order[2 + n] = jnp.transpose(orders[n]).astype(bf16)
    for ref in (va, vb):
        ref[:, 0:PAD, :] = jnp.zeros((4, PAD, HALF), f32)
        ref[:, HALF + PAD :, :] = jnp.zeros((4, PAD, HALF), f32)
    for ref in (ca, cb):
        ref[0:PAD, :] = jnp.zeros((PAD, HALF), f32)
        ref[HALF + PAD :, :] = jnp.zeros((PAD, HALF), f32)
    sc_src[...] = jnp.zeros((8, HALF), f32)

    for par in range(2):
        first.wait_recv(par)
        hartley(fh, fl, r1, par, order[par], xs, second)
        second.keep(par)
        second.wait_recv(par)
        for b in range(GROUP):
            for m in range(FEW):
                r3[par, pl.ds(m * GROUP + b, GROUP, stride=BLOCK), :] = r2[
                    par, b * BLOCK + m * GROUP : b * BLOCK + (m + 1) * GROUP, :
                ]
        if par == 0:
            third.start_all(par)
        else:
            for m in range(FEW):
                third.start_mode(par, m, 1 + m)
        third.keep(par)

    third.wait_recv(0)

    def solve_step(m, carry):
        third.wait_recv_mode(1, 1 + m)
        mode = (phi * GROUP + gz) * FEW + m
        rows = lambda zp, b: pl.ds(zp * BLOCK + m * GROUP + b, 8, stride=HALF)
        for zp in range(2):
            for b in range(GROUP):
                even, odd = even_odd(r4[0, rows(zp, b), :], r4[1, rows(zp, b), :])
                f[2 * zp, 8 * b : 8 * b + 8, :] = even
                f[2 * zp + 1, 8 * b : 8 * b + 8, :] = odd

        def write(start, values):
            for zp in range(2):
                halves = two_halves(values[2 * zp], values[2 * zp + 1])
                for g in range(CH // 8):
                    for n in range(2):
                        o4[n, rows(zp, start // 8 + g), :] = halves[n][8 * g : 8 * g + 8]

        factors = solve_mode(mode, f, base, d, w, va, vb, r, ca, cb, cr, write)
        row_ids = lax.broadcasted_iota(jnp.int32, (8, HALF), 0)
        lanes = lane_ids(8)
        for cycle in range(VCYC):
            here = (row_ids == cycle) & (lanes == gz * FEW + m)
            sc_src[...] = sc_src[...] + jnp.where(here, factors[cycle], 0.0)
        fourth.start_mode(0, m, m)
        return carry

    lax.fori_loop(0, FEW, solve_step, 0)

    for m in range(FEW):
        fourth.start_mode(1, m, FEW + m)
    fourth.keep(0)
    fourth.keep(1)

    def scale_copy(source, target, t):
        return pltpu.make_async_remote_copy(
            src_ref=source,
            dst_ref=target,
            send_sem=sc_send,
            recv_sem=sc_recv,
            device_id={"gz": t},
            device_id_type=MESH,
        )

    peers(gz, lambda t: scale_copy(sc_src, sc.at[gz], t).start())
    sc[gz] = sc_src[...]

    for par in range(2):
        for m in range(FEW):
            fourth.wait_recv_mode(par, par * FEW + m)
            for b in range(GROUP):
                p2[par, b * BLOCK + m * GROUP : b * BLOCK + (m + 1) * GROUP, :] = p3[
                    par, pl.ds(m * GROUP + b, GROUP, stride=BLOCK), :
                ]
            fifth.start_mode(par, m, par)
        fifth.keep(par)
        fifth.wait_recv(par)
        hartley(bh, bl, q1, par, order[2 + par], xs, sixth)
        sixth.keep(par)

    others = sc.at[pl.ds(0, GROUP - 1)]
    all_scales = scale_copy(others, others, lax.rem(gz + 1, GROUP))
    all_scales.wait_recv()
    total = sc[0]
    for n in range(1, GROUP):
        total = total + sc[n]
    s_ref[...] = total[:VCYC, :BLOCK]

    for exchange in (first, second, third, fourth, fifth):
        for par in range(2):
            exchange.wait_send(par)
    all_scales.wait_send()
    for par in range(2):
        sixth.wait_recv(par)
        sixth.wait_send(par)


def run(charge, outer, end, tables):
    rows = lambda: pltpu.VMEM((2, NPHI, HALF), f32)
    quad = lambda n: pltpu.VMEM((n, HALF, HALF), f32)
    table = lambda: pltpu.VMEM((NPHI, NPHI), bf16)
    whole = pl.BlockSpec(memory_space=pltpu.VMEM)
    away = pl.BlockSpec(memory_space=pl.ANY)
    return pl.pallas_call(
        main_kernel,
        out_shape=(
            jax.ShapeDtypeStruct((2, NPHI, HALF), f32),
            jax.ShapeDtypeStruct((VCYC, BLOCK), f32),
        ),
        in_specs=[away] * 7,
        out_specs=(whole, whole),
        scratch_shapes=[
            pltpu.VMEM((1, NZ), jnp.int32),
            pltpu.VMEM((1, NR), jnp.int32),
            *[rows() for _ in range(12)],
            pltpu.VMEM((4, HALF, HALF), bf16),
            pltpu.VMEM((NPHI, NR), bf16),
            table(), table(), table(), table(),
            quad(4), quad(5), quad(5), quad(4),
            pltpu.VMEM((4, HALF + 2 * PAD, HALF), f32),
            pltpu.VMEM((4, HALF + 2 * PAD, HALF), f32),
            quad(4),
            pltpu.VMEM((HALF + 2 * PAD, HALF), f32),
            pltpu.VMEM((HALF + 2 * PAD, HALF), f32),
            pltpu.VMEM((HALF, HALF), f32),
            pltpu.VMEM((8, HALF), f32),
            pltpu.VMEM((GROUP, 8, HALF), f32),
            pltpu.SemaphoreType.DMA((2,)),
            pltpu.SemaphoreType.DMA((6,)),
            pltpu.SemaphoreType.DMA((6, 2)),
            pltpu.SemaphoreType.DMA((21,)),
            pltpu.SemaphoreType.DMA,
            pltpu.SemaphoreType.DMA,
        ],
        compiler_params=pltpu.CompilerParams(
            collective_id=0, has_side_effects=True, vmem_limit_bytes=62 << 20
        ),
        name="modes",
    )(charge, outer, end, *tables)


def finish_kernel(w_ref, o_ref, rows, out, load_sem, store_sem):
    loads = [pltpu.make_async_copy(w_ref.at[half], rows.at[half], load_sem.at[half]) for half in range(2)]
    stores = [
        pltpu.make_async_copy(out.at[half], o_ref.at[:, :, pl.ds(half * HALF, HALF)], store_sem.at[half])
        for half in range(2)
    ]
    for half in range(2):
        loads[half].start()
    for half in range(2):
        loads[half].wait()
        for q in range(BLOCK):
            out[half, q] = rows[half, pl.ds(q, GROUP, stride=BLOCK), :]
        stores[half].start()
    for half in range(2):
        stores[half].wait()


def finish(w):
    return pl.pallas_call(
        finish_kernel,
        out_shape=jax.ShapeDtypeStruct((BLOCK, GROUP, NR), f32),
        in_specs=[pl.BlockSpec(memory_space=pltpu.HBM)],
        out_specs=pl.BlockSpec(memory_space=pltpu.HBM),
        scratch_shapes=[
            pltpu.VMEM((2, NPHI, HALF), f32),
            pltpu.VMEM((2, BLOCK, GROUP, HALF), f32),
            pltpu.SemaphoreType.DMA((2,)),
            pltpu.SemaphoreType.DMA((2,)),
        ],
        compiler_params=pltpu.CompilerParams(vmem_limit_bytes=63 << 20),
        name="finish",
    )(w)


def body(tables, charge, outer_held, end_held):
    hartleys = tuple(jnp.asarray(t) for t in tables)
    flat = charge.reshape(BLOCK * GROUP, NR)
    w, scales = run(flat, outer_held.reshape(1, NZ), end_held.reshape(1, NR), hartleys)
    return (finish(w), scales)


def solution(mesh):
    in_specs = (P("phi", "gz", None), P(), P())
    out_specs = (P("phi", "gz", None), P(None, "phi"))
    return jax.shard_map(
        functools.partial(body, hartley_tables()),
        mesh=mesh,
        in_specs=in_specs,
        out_specs=out_specs,
        check_vma=False,
    )
```

```python
import functools
import math

import jax
import jax.numpy as jnp
import numpy as np
from jax import lax
from jax.experimental import pallas as pl
from jax.experimental.pallas import tpu as pltpu
from jax.sharding import PartitionSpec as P

NPHI = 1024
VCYC = 2
NU = 2
KC = 3
RIN = 131
NR = 256
NZ = 256
HALF = 128
FEW = 4
GROUP = 16
BLOCK = 64
MESH = pl.DeviceIdType.MESH

relaxation = 0.8
small_floor = 1e-06
f32 = jnp.float32
bf16 = jnp.bfloat16

PAD = 8
CH = 32


def hartley_tables():
    k = np.arange(NPHI)
    phase = (np.outer(k, k) % NPHI) * (2.0 * math.pi / NPHI)
    table = ((np.cos(phase) + np.sin(phase)) / math.sqrt(NPHI)).astype(np.float32)
    order = k.reshape(GROUP, GROUP, FEW).transpose(2, 1, 0).reshape(-1)
    table = table[order]
    high = table.astype(jnp.bfloat16)
    low = (table - high.astype(np.float32)).astype(jnp.bfloat16)
    return high, low, np.ascontiguousarray(high.T), np.ascontiguousarray(low.T)


def split(values):
    high = values.astype(bf16)
    low = (values - high.astype(f32)).astype(bf16)
    return high, low


def lane_ids(rows=1):
    return lax.broadcasted_iota(jnp.int32, (rows, HALF), 1)


def fine_rows(parity):
    i = 2 * lane_ids() + parity
    radius = i.astype(f32) + (RIN + 0.5)
    inward = (radius - 0.5) / radius
    outward = (radius + 0.5) / radius
    return radius, inward, outward


def coarse_rows():
    radius = 2.0 * lane_ids().astype(f32) + (RIN + 1.0)
    inward = (radius - 1.0) / (4.0 * radius)
    outward = (radius + 1.0) / (4.0 * radius)
    return radius, inward, outward


def as_column(row):
    square = jnp.broadcast_to(row, (HALF, HALF))
    diag = lax.broadcasted_iota(jnp.int32, (HALF, HALF), 0) == lane_ids(HALF)
    return jnp.sum(jnp.where(diag, square, 0.0), axis=1, keepdims=True)


def setup_base(base_ref, outer_rows, end_rows):
    y = lax.broadcasted_iota(jnp.int32, (HALF, HALF), 0)
    j = lane_ids(HALF)
    for zp in range(2):
        open_outer = 1.0 - as_column(outer_rows[zp])
        for ip in range(2):
            _, inward, outward = fine_rows(ip)
            open_end = 1.0 - end_rows[ip]
            value = jnp.broadcast_to(inward + outward + 2.0, (HALF, HALF))
            if ip == 1:
                value = value - jnp.where(j == HALF - 1, outward * open_outer, 0.0)
            edge = 0 if zp == 0 else HALF - 1
            value = value - jnp.where(y == edge, open_end, 0.0)
            base_ref[2 * zp + ip] = value
    _, inward, outward = coarse_rows()
    open_outer = 1.0 - as_column(outer_rows[0])
    open_end = 1.0 - end_rows[0]
    value = jnp.broadcast_to(inward + outward + 0.5, (HALF, HALF))
    value = value - jnp.where(j == HALF - 1, outward * open_outer, 0.0)
    value = value - jnp.where((y == 0) | (y == HALF - 1), 0.25 * open_end, 0.0)
    base_ref[4] = value


def parity_matrix(half):
    cell = lax.broadcasted_iota(jnp.int32, (HALF, HALF), 0)
    lane = lax.broadcasted_iota(jnp.int32, (HALF, HALF), 1)
    second = (cell % 2) != half
    target = cell // 2 + jnp.where(second, HALF // 2, 0)
    return jnp.where(lane == target, 1.0, 0.0)


def even_odd(first, second):
    low = lane_ids(first.shape[0]) < HALF // 2
    even = jnp.where(low, first, second)
    odd = pltpu.roll(jnp.where(low, second, first), HALF // 2, 1)
    return even, odd


def two_halves(even, odd):
    low = lane_ids(even.shape[0]) < HALF // 2
    odd = pltpu.roll(odd, HALF // 2, 1)
    return jnp.where(low, even, odd), jnp.where(low, odd, even)


def left_of(value):
    return pltpu.roll(value, 1, 1)


def right_of(value):
    return pltpu.roll(value, HALF - 1, 1)


def solve_mode(mode, f_ref, base_ref, d_ref, w_ref, va, vb, r_ref, ca, cb, cr_ref, write):
    order = jnp.minimum(mode, NPHI - mode).astype(f32)
    square = order * order
    rows_e = fine_rows(0)
    rows_o = fine_rows(1)
    first = lane_ids() == 0
    last = lane_ids() == HALF - 1
    in_e = jnp.where(first, 0.0, rows_e[1])
    out_e = rows_e[2]
    in_o = rows_o[1]
    out_o = jnp.where(last, 0.0, rows_o[2])
    radius_c, in_c0, out_c0 = coarse_rows()
    in_c = jnp.where(first, 0.0, in_c0)
    out_c = jnp.where(last, 0.0, out_c0)
    term_e = square / (rows_e[0] * rows_e[0])
    term_o = square / (rows_o[0] * rows_o[0])
    term_c = square / (radius_c * radius_c)
    chunks = [pl.ds(s, CH) for s in range(0, HALF, CH)]
    padded = [pl.ds(PAD + s, CH) for s in range(0, HALF, CH)]
    above = [pl.ds(PAD + s - 1, CH) for s in range(0, HALF, CH)]
    below = [pl.ds(PAD + s + 1, CH) for s in range(0, HALF, CH)]
    count = len(chunks)

    def neighbours(v, c):
        ee, eo, oe, oo = (v[q, padded[c], :] for q in range(4))
        oe_up, oo_up = v[2, above[c], :], v[3, above[c], :]
        ee_dn, eo_dn = v[0, below[c], :], v[1, below[c], :]
        n_ee = (oe_up + oe) + (in_e * left_of(eo) + out_e * eo)
        n_eo = (oo_up + oo) + (in_o * ee + out_o * right_of(ee))
        n_oe = (ee + ee_dn) + (in_e * left_of(oo) + out_e * oo)
        n_oo = (eo + eo_dn) + (in_o * oe + out_o * right_of(oe))
        return (ee, eo, oe, oo), (n_ee, n_eo, n_oe, n_oo)

    def sweep(src, dst, emit=None):
        for c in range(count):
            centre, near = neighbours(src, c)
            values = []
            for q in range(4):
                value = (1.0 - relaxation) * centre[q] + w_ref[q, chunks[c], :] * (
                    f_ref[q, chunks[c], :] + near[q]
                )
                if emit is None:
                    dst[q, padded[c], :] = value
                values.append(value)
            if emit is not None:
                emit(c * CH, values)

    for c in range(count):
        for q in range(4):
            d = base_ref[q, chunks[c], :] + (term_e if q % 2 == 0 else term_o)
            w = relaxation / d
            d_ref[q, chunks[c], :] = d
            w_ref[q, chunks[c], :] = w
            va[q, padded[c], :] = w * f_ref[q, chunks[c], :]
        d_ref[4, chunks[c], :] = relaxation / (base_ref[4, chunks[c], :] + term_c)

    factors = []
    cur, other = va, vb
    for cycle in range(VCYC):
        for s in range(1 if cycle == 0 else 0, NU):
            sweep(cur, other)
            cur, other = other, cur
        for c in range(count):
            centre, near = neighbours(cur, c)
            total = None
            for q in range(4):
                res = f_ref[q, chunks[c], :] + near[q] - d_ref[q, chunks[c], :] * centre[q]
                r_ref[q, chunks[c], :] = res
                total = res if total is None else total + res
            total = total * 0.25
            cr_ref[chunks[c], :] = total
            ca[padded[c], :] = d_ref[4, chunks[c], :] * total
        now, later = ca, cb
        for s in range(KC):
            for c in range(count):
                w = now[padded[c], :]
                near = (
                    in_c * left_of(w)
                    + out_c * right_of(w)
                    + 0.25 * (now[above[c], :] + now[below[c], :])
                )
                later[padded[c], :] = (1.0 - relaxation) * w + d_ref[4, chunks[c], :] * (
                    cr_ref[chunks[c], :] + near
                )
            now, later = later, now
        top = jnp.zeros((8, HALF), f32)
        bottom = jnp.zeros((8, HALF), f32)
        for c in range(count):
            w = now[padded[c], :]
            low_e = in_e * left_of(w) + out_e * w
            low_o = in_o * w + out_o * right_of(w)
            up = now[above[c], :] + w
            down = now[below[c], :] + w
            for q in range(4):
                image = d_ref[q, chunks[c], :] * w - (low_e if q % 2 == 0 else low_o)
                image = image - (up if q < 2 else down)
                res = r_ref[q, chunks[c], :]
                for g in range(CH // 8):
                    part = image[8 * g : 8 * g + 8]
                    top = top + res[8 * g : 8 * g + 8] * part
                    bottom = bottom + part * part
        factor = jnp.sum(top, keepdims=True) / (jnp.sum(bottom, keepdims=True) + small_floor)
        factors.append(factor)
        for c in range(count):
            add = factor * now[padded[c], :]
            for q in range(4):
                cur[q, padded[c], :] = cur[q, padded[c], :] + add
        for s in range(NU):
            if cycle == VCYC - 1 and s == NU - 1:
                sweep(cur, None, write)
            else:
                sweep(cur, other)
                cur, other = other, cur
    return factors


def block(index):
    return pl.ds(pl.multiple_of(index * BLOCK, BLOCK), BLOCK)


def peers(me, action):
    def step(n, carry):
        away = (n // 2 + 1) * (1 - 2 * lax.rem(n, 2))
        action(lax.rem(me + GROUP + away, GROUP))
        return carry

    lax.fori_loop(0, GROUP - 1, step, 0)


class Exchange:
    def __init__(self, axis, src, dst, send, recv, base, by_mode=False):
        self.axis, self.src, self.dst, self.send, self.recv = axis, src, dst, send, recv
        self.base, self.by_mode = base, by_mode
        self.me = lax.axis_index(axis)

    def copy(self, par, source, target, t, sem):
        return pltpu.make_async_remote_copy(
            src_ref=self.src.at[par, source],
            dst_ref=self.dst.at[par, target],
            send_sem=self.send.at[par],
            recv_sem=self.recv.at[self.base + sem],
            device_id={self.axis: t},
            device_id_type=MESH,
        )

    def place(self, t, m):
        if self.by_mode:
            return pl.ds(pl.multiple_of(m * (GROUP * GROUP) + t * GROUP, GROUP), GROUP)
        return pl.ds(pl.multiple_of(t * BLOCK + m * GROUP, GROUP), GROUP)

    def start(self, par, t):
        self.copy(par, block(t), block(self.me), t, par).start()

    def start_mode(self, par, m, sem):
        peers(
            self.me,
            lambda t: self.copy(par, self.place(t, m), self.place(self.me, m), t, sem).start(),
        )

    def keep(self, par):
        for m in range(FEW):
            here = self.place(self.me, m)
            self.dst[par, here, :] = self.src[par, here, :]

    def whole(self, par, rows, sem):
        t = lax.rem(self.me + 1, GROUP)
        return self.copy(par, pl.ds(0, rows), pl.ds(0, rows), t, sem)

    def wait_recv(self, par):
        self.whole(par, (GROUP - 1) * BLOCK, par).wait_recv()

    def wait_recv_mode(self, par, sem):
        self.whole(par, (GROUP - 1) * GROUP, sem).wait_recv()

    def wait_send(self, par):
        self.whole(par, (GROUP - 1) * BLOCK, par).wait_send()


def hartley(high, low, src, dst, par, order, xs, first, ready):
    for piece in range(4):
        rows = pl.ds(piece * 256, 256)
        h, l = split(src[par, rows, :])
        xs[rows, :HALF] = jnp.dot(h, order, preferred_element_type=f32).astype(bf16)
        xs[rows, HALF:] = jnp.dot(l, order, preferred_element_type=f32).astype(bf16)
    def step(n, carry):
        piece = lax.rem(first + n, 4)
        rows = pl.ds(pl.multiple_of(piece * 256, 256), 256)
        both = jnp.dot(high[rows, :], xs[...], preferred_element_type=f32)
        rest = jnp.dot(low[rows, :], xs[:, :HALF], preferred_element_type=f32)
        dst[par, rows, :] = both[:, :HALF] + (both[:, HALF:] + rest)
        ready(piece)
        return carry

    lax.fori_loop(0, 4, step, 0)


def main_kernel(
    charge_ref, outer_ref, end_ref, fh_ref, fl_ref, bh_ref, bl_ref,
    w_ref, s_ref,
    outer, end, xin, t1, r1, s1, r2, r3, r4, o4, p3, p2, q1, v1, order, xs,
    fh, fl, bh, bl,
    f, base, d, w, va, vb, r, ca, cb, cr, sc_src, sc,
    in_sem, table_sem, send, recv, sc_send, sc_recv,
):
    phi, gz = lax.axis_index("phi"), lax.axis_index("gz")
    loads = [
        pltpu.make_async_copy(charge_ref.at[:, pl.ds(half * HALF, HALF)], xin.at[half], in_sem.at[half])
        for half in range(2)
    ]
    for copy in loads:
        copy.start()
    tables = [
        pltpu.make_async_copy(src, dst, table_sem.at[n])
        for n, (src, dst) in enumerate(((outer_ref, outer), (end_ref, end), (fh_ref, fh), (fl_ref, fl), (bh_ref, bh), (bl_ref, bl)))
    ]
    for copy in tables:
        copy.start()
    barrier = pltpu.get_barrier_semaphore()
    for axis, me in (("phi", phi), ("gz", gz)):
        peers(
            me,
            lambda t: pl.semaphore_signal(barrier, inc=1, device_id={axis: t}, device_id_type=MESH),
        )

    first = Exchange("phi", t1, r1, send.at[0], recv, 0)
    second = Exchange("gz", s1, r2, send.at[1], recv, 2, True)
    third = Exchange("phi", r3, r4, send.at[2], recv, 10)
    fourth = Exchange("phi", o4, p3, send.at[3], recv, 15)
    fifth = Exchange("gz", p2, q1, send.at[4], recv, 23, True)
    sixth = Exchange("phi", v1, w_ref, send.at[5], recv, 25)

    for half in range(2):
        loads[half].wait()
        if half == 0:
            pl.semaphore_wait(barrier, 2 * (GROUP - 1))

        def regroup(t):
            t1[half, block(t), :] = xin[half, pl.ds(t, BLOCK, stride=GROUP), :]
            first.start(half, t)

        peers(phi, regroup)
        r1[half, block(phi), :] = xin[half, pl.ds(phi, BLOCK, stride=GROUP), :]

    for copy in tables:
        copy.wait()
    orders = [parity_matrix(0), parity_matrix(1)]
    held = jnp.concatenate([outer[...]] * 4 + [end[...]] * 4, axis=0).astype(f32)
    held = even_odd(*(
        jnp.dot(
            held[:, n * HALF : (n + 1) * HALF].astype(bf16),
            orders[n].astype(bf16),
            preferred_element_type=f32,
        )
        for n in range(2)
    ))
    setup_base(base, [row[0:1] for row in held], [row[4:5] for row in held])
    for n in range(2):
        order[n] = orders[n].astype(bf16)
        order[2 + n] = jnp.transpose(orders[n]).astype(bf16)
    for ref in (va, vb):
        ref[:, 0:PAD, :] = jnp.zeros((4, PAD, HALF), f32)
        ref[:, HALF + PAD :, :] = jnp.zeros((4, PAD, HALF), f32)
    for ref in (ca, cb):
        ref[0:PAD, :] = jnp.zeros((PAD, HALF), f32)
        ref[HALF + PAD :, :] = jnp.zeros((PAD, HALF), f32)
    sc_src[...] = jnp.zeros((8, HALF), f32)

    for par in range(2):
        first.wait_recv(par)
        hartley(
            fh, fl, r1, s1, par, order[par], xs, 0,
            lambda m: second.start_mode(par, m, par * FEW + m),
        )
        second.keep(par)

        def forward(m, carry):
            second.wait_recv_mode(par, par * FEW + m)
            for b in range(GROUP):
                r3[par, pl.ds(m * GROUP + b, GROUP, stride=BLOCK), :] = r2[
                    par, pl.ds(pl.multiple_of(m * (GROUP * GROUP) + b * GROUP, GROUP), GROUP), :
                ]
            third.start_mode(par, m, par * (1 + m))
            return carry

        lax.fori_loop(0, FEW, forward, 0)
        third.keep(par)

    third.wait_recv(0)

    def solve_step(m, carry):
        third.wait_recv_mode(1, 1 + m)
        mode = (phi * GROUP + gz) * FEW + m
        rows = lambda zp, b: pl.ds(zp * BLOCK + m * GROUP + b, 8, stride=HALF)
        for zp in range(2):
            for b in range(GROUP):
                even, odd = even_odd(r4[0, rows(zp, b), :], r4[1, rows(zp, b), :])
                f[2 * zp, 8 * b : 8 * b + 8, :] = even
                f[2 * zp + 1, 8 * b : 8 * b + 8, :] = odd

        def write(start, values):
            for zp in range(2):
                halves = two_halves(values[2 * zp], values[2 * zp + 1])
                for g in range(CH // 8):
                    for n in range(2):
                        o4[n, rows(zp, start // 8 + g), :] = halves[n][8 * g : 8 * g + 8]

        factors = solve_mode(mode, f, base, d, w, va, vb, r, ca, cb, cr, write)
        row_ids = lax.broadcasted_iota(jnp.int32, (8, HALF), 0)
        lanes = lane_ids(8)
        for cycle in range(VCYC):
            here = (row_ids == cycle) & (lanes == gz * FEW + m)
            sc_src[...] = sc_src[...] + jnp.where(here, factors[cycle], 0.0)
        fourth.start_mode(0, m, m)
        return carry

    lax.fori_loop(0, FEW, solve_step, 0)

    for m in range(FEW):
        fourth.start_mode(1, m, FEW + m)
    fourth.keep(0)
    fourth.keep(1)

    def scale_copy(source, target, t):
        return pltpu.make_async_remote_copy(
            src_ref=source,
            dst_ref=target,
            send_sem=sc_send,
            recv_sem=sc_recv,
            device_id={"gz": t},
            device_id_type=MESH,
        )

    peers(gz, lambda t: scale_copy(sc_src, sc.at[gz], t).start())
    sc[gz] = sc_src[...]

    def send_quarter(par, piece):
        for n in range(4):
            t = piece * 4 + lax.rem(phi + n, 4)

            @pl.when(t != phi)
            def _():
                sixth.start(par, t)

    for par in range(2):

        def backward(m, carry):
            fourth.wait_recv_mode(par, par * FEW + m)
            for b in range(GROUP):
                p2[par, pl.ds(pl.multiple_of(m * (GROUP * GROUP) + b * GROUP, GROUP), GROUP), :] = p3[
                    par, pl.ds(m * GROUP + b, GROUP, stride=BLOCK), :
                ]
            fifth.start_mode(par, m, par)
            return carry

        lax.fori_loop(0, FEW, backward, 0)
        fifth.keep(par)
        fifth.wait_recv(par)
        hartley(
            bh, bl, q1, v1, par, order[2 + par], xs, phi // 4, lambda piece: send_quarter(par, piece)
        )
        sixth.keep(par)

    others = sc.at[pl.ds(0, GROUP - 1)]
    all_scales = scale_copy(others, others, lax.rem(gz + 1, GROUP))
    all_scales.wait_recv()
    total = sc[0]
    for n in range(1, GROUP):
        total = total + sc[n]
    s_ref[...] = total[:VCYC, :BLOCK]

    for exchange in (first, second, third, fourth, fifth):
        for par in range(2):
            exchange.wait_send(par)
    all_scales.wait_send()
    for par in range(2):
        sixth.wait_recv(par)
        sixth.wait_send(par)


def run(charge, outer, end, tables):
    rows = lambda: pltpu.VMEM((2, NPHI, HALF), f32)
    quad = lambda n: pltpu.VMEM((n, HALF, HALF), f32)
    table = lambda: pltpu.VMEM((NPHI, NPHI), bf16)
    whole = pl.BlockSpec(memory_space=pltpu.VMEM)
    away = pl.BlockSpec(memory_space=pl.ANY)
    return pl.pallas_call(
        main_kernel,
        out_shape=(
            jax.ShapeDtypeStruct((2, NPHI, HALF), f32),
            jax.ShapeDtypeStruct((VCYC, BLOCK), f32),
        ),
        in_specs=[away] * 7,
        out_specs=(whole, whole),
        scratch_shapes=[
            pltpu.VMEM((1, NZ), jnp.int32),
            pltpu.VMEM((1, NR), jnp.int32),
            *[rows() for _ in range(12)],
            pltpu.VMEM((4, HALF, HALF), bf16),
            pltpu.VMEM((NPHI, NR), bf16),
            table(), table(), table(), table(),
            quad(4), quad(5), quad(5), quad(4),
            pltpu.VMEM((4, HALF + 2 * PAD, HALF), f32),
            pltpu.VMEM((4, HALF + 2 * PAD, HALF), f32),
            quad(4),
            pltpu.VMEM((HALF + 2 * PAD, HALF), f32),
            pltpu.VMEM((HALF + 2 * PAD, HALF), f32),
            pltpu.VMEM((HALF, HALF), f32),
            pltpu.VMEM((8, HALF), f32),
            pltpu.VMEM((GROUP, 8, HALF), f32),
            pltpu.SemaphoreType.DMA((2,)),
            pltpu.SemaphoreType.DMA((6,)),
            pltpu.SemaphoreType.DMA((6, 2)),
            pltpu.SemaphoreType.DMA((27,)),
            pltpu.SemaphoreType.DMA,
            pltpu.SemaphoreType.DMA,
        ],
        compiler_params=pltpu.CompilerParams(
            collective_id=0, has_side_effects=True, vmem_limit_bytes=62 << 20
        ),
        name="modes",
    )(charge, outer, end, *tables)


def finish_kernel(w_ref, o_ref, rows, out, load_sem, store_sem):
    loads = [pltpu.make_async_copy(w_ref.at[half], rows.at[half], load_sem.at[half]) for half in range(2)]
    stores = [
        pltpu.make_async_copy(out.at[half], o_ref.at[:, :, pl.ds(half * HALF, HALF)], store_sem.at[half])
        for half in range(2)
    ]
    for half in range(2):
        loads[half].start()
    for half in range(2):
        loads[half].wait()
        for q in range(BLOCK):
            out[half, q] = rows[half, pl.ds(q, GROUP, stride=BLOCK), :]
        stores[half].start()
    for half in range(2):
        stores[half].wait()


def finish(w):
    return pl.pallas_call(
        finish_kernel,
        out_shape=jax.ShapeDtypeStruct((BLOCK, GROUP, NR), f32),
        in_specs=[pl.BlockSpec(memory_space=pltpu.HBM)],
        out_specs=pl.BlockSpec(memory_space=pltpu.HBM),
        scratch_shapes=[
            pltpu.VMEM((2, NPHI, HALF), f32),
            pltpu.VMEM((2, BLOCK, GROUP, HALF), f32),
            pltpu.SemaphoreType.DMA((2,)),
            pltpu.SemaphoreType.DMA((2,)),
        ],
        compiler_params=pltpu.CompilerParams(vmem_limit_bytes=63 << 20),
        name="finish",
    )(w)


def body(tables, charge, outer_held, end_held):
    hartleys = tuple(jnp.asarray(t) for t in tables)
    flat = charge.reshape(BLOCK * GROUP, NR)
    w, scales = run(flat, outer_held.reshape(1, NZ), end_held.reshape(1, NR), hartleys)
    return (finish(w), scales)


def solution(mesh):
    in_specs = (P("phi", "gz", None), P(), P())
    out_specs = (P("phi", "gz", None), P(None, "phi"))
    return jax.shard_map(
        functools.partial(body, hartley_tables()),
        mesh=mesh,
        in_specs=in_specs,
        out_specs=out_specs,
        check_vma=False,
    )
```

```python
import functools
import math

import jax
import jax.numpy as jnp
import numpy as np
from jax import lax
from jax.experimental import pallas as pl
from jax.experimental.pallas import tpu as pltpu
from jax.sharding import PartitionSpec as P

NPHI = 1024
VCYC = 2
NU = 2
KC = 3
RIN = 131
NR = 256
NZ = 256
HALF = 128
FEW = 4
GROUP = 16
BLOCK = 64
MESH = pl.DeviceIdType.MESH

relaxation = 0.8
small_floor = 1e-06
f32 = jnp.float32
bf16 = jnp.bfloat16

PAD = 8
CH = 32


def hartley_tables():
    k = np.arange(NPHI)
    phase = (np.outer(k, k) % NPHI) * (2.0 * math.pi / NPHI)
    table = ((np.cos(phase) + np.sin(phase)) / math.sqrt(NPHI)).astype(np.float32)
    order = k.reshape(GROUP, GROUP, FEW).transpose(2, 1, 0).reshape(-1)
    table = table[order]
    high = table.astype(jnp.bfloat16)
    low = (table - high.astype(np.float32)).astype(jnp.bfloat16)
    return high, low, np.ascontiguousarray(high.T), np.ascontiguousarray(low.T)


def split(values):
    high = values.astype(bf16)
    low = (values - high.astype(f32)).astype(bf16)
    return high, low


def lane_ids(rows=1):
    return lax.broadcasted_iota(jnp.int32, (rows, HALF), 1)


def fine_rows(parity):
    i = 2 * lane_ids() + parity
    radius = i.astype(f32) + (RIN + 0.5)
    inward = (radius - 0.5) / radius
    outward = (radius + 0.5) / radius
    return radius, inward, outward


def coarse_rows():
    radius = 2.0 * lane_ids().astype(f32) + (RIN + 1.0)
    inward = (radius - 1.0) / (4.0 * radius)
    outward = (radius + 1.0) / (4.0 * radius)
    return radius, inward, outward


def as_column(row):
    square = jnp.broadcast_to(row, (HALF, HALF))
    diag = lax.broadcasted_iota(jnp.int32, (HALF, HALF), 0) == lane_ids(HALF)
    return jnp.sum(jnp.where(diag, square, 0.0), axis=1, keepdims=True)


def setup_base(base_ref, outer_rows, end_rows):
    y = lax.broadcasted_iota(jnp.int32, (HALF, HALF), 0)
    j = lane_ids(HALF)
    for zp in range(2):
        open_outer = 1.0 - as_column(outer_rows[zp])
        for ip in range(2):
            _, inward, outward = fine_rows(ip)
            open_end = 1.0 - end_rows[ip]
            value = jnp.broadcast_to(inward + outward + 2.0, (HALF, HALF))
            if ip == 1:
                value = value - jnp.where(j == HALF - 1, outward * open_outer, 0.0)
            edge = 0 if zp == 0 else HALF - 1
            value = value - jnp.where(y == edge, open_end, 0.0)
            base_ref[2 * zp + ip] = value
    _, inward, outward = coarse_rows()
    open_outer = 1.0 - as_column(outer_rows[0])
    open_end = 1.0 - end_rows[0]
    value = jnp.broadcast_to(inward + outward + 0.5, (HALF, HALF))
    value = value - jnp.where(j == HALF - 1, outward * open_outer, 0.0)
    value = value - jnp.where((y == 0) | (y == HALF - 1), 0.25 * open_end, 0.0)
    base_ref[4] = value


def parity_matrix(half):
    cell = lax.broadcasted_iota(jnp.int32, (HALF, HALF), 0)
    lane = lax.broadcasted_iota(jnp.int32, (HALF, HALF), 1)
    second = (cell % 2) != half
    target = cell // 2 + jnp.where(second, HALF // 2, 0)
    return jnp.where(lane == target, 1.0, 0.0)


def even_odd(first, second):
    low = lane_ids(first.shape[0]) < HALF // 2
    even = jnp.where(low, first, second)
    odd = pltpu.roll(jnp.where(low, second, first), HALF // 2, 1)
    return even, odd


def two_halves(even, odd):
    low = lane_ids(even.shape[0]) < HALF // 2
    odd = pltpu.roll(odd, HALF // 2, 1)
    return jnp.where(low, even, odd), jnp.where(low, odd, even)


def left_of(value):
    return pltpu.roll(value, 1, 1)


def right_of(value):
    return pltpu.roll(value, HALF - 1, 1)


def solve_mode(mode, f_ref, base_ref, d_ref, w_ref, va, vb, r_ref, ca, cb, cr_ref, write):
    order = jnp.minimum(mode, NPHI - mode).astype(f32)
    square = order * order
    rows_e = fine_rows(0)
    rows_o = fine_rows(1)
    first = lane_ids() == 0
    last = lane_ids() == HALF - 1
    in_e = jnp.where(first, 0.0, rows_e[1])
    out_e = rows_e[2]
    in_o = rows_o[1]
    out_o = jnp.where(last, 0.0, rows_o[2])
    radius_c, in_c0, out_c0 = coarse_rows()
    in_c = jnp.where(first, 0.0, in_c0)
    out_c = jnp.where(last, 0.0, out_c0)
    term_e = square / (rows_e[0] * rows_e[0])
    term_o = square / (rows_o[0] * rows_o[0])
    term_c = square / (radius_c * radius_c)
    chunks = [pl.ds(s, CH) for s in range(0, HALF, CH)]
    padded = [pl.ds(PAD + s, CH) for s in range(0, HALF, CH)]
    above = [pl.ds(PAD + s - 1, CH) for s in range(0, HALF, CH)]
    below = [pl.ds(PAD + s + 1, CH) for s in range(0, HALF, CH)]
    count = len(chunks)

    def neighbours(v, c):
        ee, eo, oe, oo = (v[q, padded[c], :] for q in range(4))
        oe_up, oo_up = v[2, above[c], :], v[3, above[c], :]
        ee_dn, eo_dn = v[0, below[c], :], v[1, below[c], :]
        n_ee = (oe_up + oe) + (in_e * left_of(eo) + out_e * eo)
        n_eo = (oo_up + oo) + (in_o * ee + out_o * right_of(ee))
        n_oe = (ee + ee_dn) + (in_e * left_of(oo) + out_e * oo)
        n_oo = (eo + eo_dn) + (in_o * oe + out_o * right_of(oe))
        return (ee, eo, oe, oo), (n_ee, n_eo, n_oe, n_oo)

    def sweep(src, dst, emit=None):
        for c in range(count):
            centre, near = neighbours(src, c)
            values = []
            for q in range(4):
                value = (1.0 - relaxation) * centre[q] + w_ref[q, chunks[c], :] * (
                    f_ref[q, chunks[c], :] + near[q]
                )
                if emit is None:
                    dst[q, padded[c], :] = value
                values.append(value)
            if emit is not None:
                emit(c * CH, values)

    for c in range(count):
        for q in range(4):
            d = base_ref[q, chunks[c], :] + (term_e if q % 2 == 0 else term_o)
            w = relaxation / d
            d_ref[q, chunks[c], :] = d
            w_ref[q, chunks[c], :] = w
            va[q, padded[c], :] = w * f_ref[q, chunks[c], :]
        d_ref[4, chunks[c], :] = relaxation / (base_ref[4, chunks[c], :] + term_c)

    factors = []
    cur, other = va, vb
    for cycle in range(VCYC):
        for s in range(1 if cycle == 0 else 0, NU):
            sweep(cur, other)
            cur, other = other, cur
        for c in range(count):
            centre, near = neighbours(cur, c)
            total = None
            for q in range(4):
                res = f_ref[q, chunks[c], :] + near[q] - d_ref[q, chunks[c], :] * centre[q]
                r_ref[q, chunks[c], :] = res
                total = res if total is None else total + res
            total = total * 0.25
            cr_ref[chunks[c], :] = total
            ca[padded[c], :] = d_ref[4, chunks[c], :] * total
        now, later = ca, cb
        for s in range(KC):
            for c in range(count):
                w = now[padded[c], :]
                near = (
                    in_c * left_of(w)
                    + out_c * right_of(w)
                    + 0.25 * (now[above[c], :] + now[below[c], :])
                )
                later[padded[c], :] = (1.0 - relaxation) * w + d_ref[4, chunks[c], :] * (
                    cr_ref[chunks[c], :] + near
                )
            now, later = later, now
        top = jnp.zeros((8, HALF), f32)
        bottom = jnp.zeros((8, HALF), f32)
        for c in range(count):
            w = now[padded[c], :]
            low_e = in_e * left_of(w) + out_e * w
            low_o = in_o * w + out_o * right_of(w)
            up = now[above[c], :] + w
            down = now[below[c], :] + w
            for q in range(4):
                image = d_ref[q, chunks[c], :] * w - (low_e if q % 2 == 0 else low_o)
                image = image - (up if q < 2 else down)
                res = r_ref[q, chunks[c], :]
                for g in range(CH // 8):
                    part = image[8 * g : 8 * g + 8]
                    top = top + res[8 * g : 8 * g + 8] * part
                    bottom = bottom + part * part
        factor = jnp.sum(top, keepdims=True) / (jnp.sum(bottom, keepdims=True) + small_floor)
        factors.append(factor)
        for c in range(count):
            add = factor * now[padded[c], :]
            for q in range(4):
                cur[q, padded[c], :] = cur[q, padded[c], :] + add
        for s in range(NU):
            if cycle == VCYC - 1 and s == NU - 1:
                sweep(cur, None, write)
            else:
                sweep(cur, other)
                cur, other = other, cur
    return factors


def block(index):
    return pl.ds(pl.multiple_of(index * BLOCK, BLOCK), BLOCK)


def far_peers(me, action):
    def step(n, carry):
        away = (GROUP // 2 - (n + 1) // 2) * (1 - 2 * lax.rem(n, 2))
        action(lax.rem(me + GROUP + away, GROUP))
        return carry

    lax.fori_loop(0, GROUP - 1, step, 0)


def peers(me, action):
    def step(n, carry):
        away = (n // 2 + 1) * (1 - 2 * lax.rem(n, 2))
        action(lax.rem(me + GROUP + away, GROUP))
        return carry

    lax.fori_loop(0, GROUP - 1, step, 0)


class Exchange:
    def __init__(self, axis, src, dst, send, recv, base, by_mode=False):
        self.axis, self.src, self.dst, self.send, self.recv = axis, src, dst, send, recv
        self.base, self.by_mode = base, by_mode
        self.me = lax.axis_index(axis)

    def copy(self, par, source, target, t, sem):
        return pltpu.make_async_remote_copy(
            src_ref=self.src.at[par, source],
            dst_ref=self.dst.at[par, target],
            send_sem=self.send.at[par],
            recv_sem=self.recv.at[self.base + sem],
            device_id={self.axis: t},
            device_id_type=MESH,
        )

    def place(self, t, m):
        if self.by_mode:
            return pl.ds(pl.multiple_of(m * (GROUP * GROUP) + t * GROUP, GROUP), GROUP)
        return pl.ds(pl.multiple_of(t * BLOCK + m * GROUP, GROUP), GROUP)

    def start(self, par, t):
        self.copy(par, block(t), block(self.me), t, par).start()

    def start_mode(self, par, m, sem):
        peers(
            self.me,
            lambda t: self.copy(par, self.place(t, m), self.place(self.me, m), t, sem).start(),
        )

    def keep(self, par):
        for m in range(FEW):
            here = self.place(self.me, m)
            self.dst[par, here, :] = self.src[par, here, :]

    def whole(self, par, rows, sem):
        t = lax.rem(self.me + 1, GROUP)
        return self.copy(par, pl.ds(0, rows), pl.ds(0, rows), t, sem)

    def wait_recv(self, par):
        self.whole(par, (GROUP - 1) * BLOCK, par).wait_recv()

    def wait_recv_mode(self, par, sem):
        self.whole(par, (GROUP - 1) * GROUP, sem).wait_recv()

    def wait_send(self, par):
        self.whole(par, (GROUP - 1) * BLOCK, par).wait_send()


def hartley(high, low, src, dst, par, order, xs, first, ready):
    for piece in range(4):
        rows = pl.ds(piece * 256, 256)
        h, l = split(src[par, rows, :])
        xs[rows, :HALF] = jnp.dot(h, order, preferred_element_type=f32).astype(bf16)
        xs[rows, HALF:] = jnp.dot(l, order, preferred_element_type=f32).astype(bf16)
    def step(n, carry):
        piece = lax.rem(first + n, 4)
        rows = pl.ds(pl.multiple_of(piece * 256, 256), 256)
        both = jnp.dot(high[rows, :], xs[...], preferred_element_type=f32)
        rest = jnp.dot(low[rows, :], xs[:, :HALF], preferred_element_type=f32)
        dst[par, rows, :] = both[:, :HALF] + (both[:, HALF:] + rest)
        ready(piece)
        return carry

    lax.fori_loop(0, 4, step, 0)


def main_kernel(
    charge_ref, outer_ref, end_ref, fh_ref, fl_ref, bh_ref, bl_ref,
    w_ref, s_ref,
    outer, end, r1, s1, r2, r3, r4, o4, p3, p2, q1, v1, order, xs,
    fh, fl, bh, bl,
    f, base, d, w, va, vb, r, ca, cb, cr, sc_src, sc,
    in_sem, table_sem, keep_sem, send, recv, sc_send, sc_recv,
):
    phi, gz = lax.axis_index("phi"), lax.axis_index("gz")
    own_loads = [
        pltpu.make_async_copy(
            charge_ref.at[:, phi, pl.ds(half * HALF, HALF)], r1.at[half, block(phi)], in_sem.at[half]
        )
        for half in range(2)
    ]
    tables = [
        pltpu.make_async_copy(src, dst, table_sem.at[n])
        for n, (src, dst) in enumerate(((outer_ref, outer), (end_ref, end), (fh_ref, fh), (fl_ref, fl), (bh_ref, bh), (bl_ref, bl)))
    ]
    barrier = pltpu.get_barrier_semaphore()
    for axis, me in (("phi", phi), ("gz", gz)):
        peers(
            me,
            lambda t: pl.semaphore_signal(barrier, inc=1, device_id={axis: t}, device_id_type=MESH),
        )

    first = Exchange("phi", s1, r1, send.at[0], recv, 0)
    second = Exchange("gz", s1, r2, send.at[1], recv, 2, True)
    third = Exchange("phi", r3, r4, send.at[2], recv, 10)
    fourth = Exchange("phi", o4, p3, send.at[3], recv, 15)
    fifth = Exchange("gz", p2, q1, send.at[4], recv, 23, True)
    sixth = Exchange("phi", v1, q1, send.at[5], recv, 25)

    pl.semaphore_wait(barrier, 2 * (GROUP - 1))

    def first_copy(half, t):
        return pltpu.make_async_remote_copy(
            src_ref=charge_ref.at[:, t, pl.ds(half * HALF, HALF)],
            dst_ref=r1.at[half, block(phi)],
            send_sem=send.at[0, half],
            recv_sem=recv.at[half],
            device_id={"phi": t},
            device_id_type=MESH,
        )

    for half in range(2):
        far_peers(phi, lambda t: first_copy(half, t).start())
        own_loads[half].start()
    for copy in tables:
        copy.start()

    for copy in tables:
        copy.wait()
    orders = [parity_matrix(0), parity_matrix(1)]
    held = jnp.concatenate([outer[...]] * 4 + [end[...]] * 4, axis=0).astype(f32)
    held = even_odd(*(
        jnp.dot(
            held[:, n * HALF : (n + 1) * HALF].astype(bf16),
            orders[n].astype(bf16),
            preferred_element_type=f32,
        )
        for n in range(2)
    ))
    setup_base(base, [row[0:1] for row in held], [row[4:5] for row in held])
    for n in range(2):
        order[n] = orders[n].astype(bf16)
        order[2 + n] = jnp.transpose(orders[n]).astype(bf16)
    for ref in (va, vb):
        ref[:, 0:PAD, :] = jnp.zeros((4, PAD, HALF), f32)
        ref[:, HALF + PAD :, :] = jnp.zeros((4, PAD, HALF), f32)
    for ref in (ca, cb):
        ref[0:PAD, :] = jnp.zeros((PAD, HALF), f32)
        ref[HALF + PAD :, :] = jnp.zeros((PAD, HALF), f32)
    sc_src[...] = jnp.zeros((8, HALF), f32)

    for par in range(2):
        first.wait_recv(par)
        own_loads[par].wait()
        hartley(
            fh, fl, r1, s1, par, order[par], xs, 0,
            lambda m: second.start_mode(par, m, par * FEW + m),
        )
        second.keep(par)

        def forward(m, carry):
            second.wait_recv_mode(par, par * FEW + m)
            for b in range(GROUP):
                r3[par, pl.ds(m * GROUP + b, GROUP, stride=BLOCK), :] = r2[
                    par, pl.ds(pl.multiple_of(m * (GROUP * GROUP) + b * GROUP, GROUP), GROUP), :
                ]
            third.start_mode(par, m, par * (1 + m))
            return carry

        lax.fori_loop(0, FEW, forward, 0)
        third.keep(par)

    third.wait_recv(0)

    def solve_step(m, carry):
        third.wait_recv_mode(1, 1 + m)
        mode = (phi * GROUP + gz) * FEW + m
        rows = lambda zp, b: pl.ds(zp * BLOCK + m * GROUP + b, 8, stride=HALF)
        for zp in range(2):
            for b in range(GROUP):
                even, odd = even_odd(r4[0, rows(zp, b), :], r4[1, rows(zp, b), :])
                f[2 * zp, 8 * b : 8 * b + 8, :] = even
                f[2 * zp + 1, 8 * b : 8 * b + 8, :] = odd

        def write(start, values):
            for zp in range(2):
                halves = two_halves(values[2 * zp], values[2 * zp + 1])
                for g in range(CH // 8):
                    for n in range(2):
                        o4[n, rows(zp, start // 8 + g), :] = halves[n][8 * g : 8 * g + 8]

        factors = solve_mode(mode, f, base, d, w, va, vb, r, ca, cb, cr, write)
        row_ids = lax.broadcasted_iota(jnp.int32, (8, HALF), 0)
        lanes = lane_ids(8)
        for cycle in range(VCYC):
            here = (row_ids == cycle) & (lanes == gz * FEW + m)
            sc_src[...] = sc_src[...] + jnp.where(here, factors[cycle], 0.0)
        fourth.start_mode(0, m, m)
        return carry

    lax.fori_loop(0, FEW, solve_step, 0)

    for m in range(FEW):
        fourth.start_mode(1, m, FEW + m)
    fourth.keep(0)
    fourth.keep(1)

    def scale_copy(source, target, t):
        return pltpu.make_async_remote_copy(
            src_ref=source,
            dst_ref=target,
            send_sem=sc_send,
            recv_sem=sc_recv,
            device_id={"gz": t},
            device_id_type=MESH,
        )

    peers(gz, lambda t: scale_copy(sc_src, sc.at[gz], t).start())
    sc[gz] = sc_src[...]

    def last_copy(par, t):
        return pltpu.make_async_remote_copy(
            src_ref=v1.at[par, block(t)],
            dst_ref=w_ref.at[:, phi, pl.ds(par * HALF, HALF)],
            send_sem=send.at[5, par],
            recv_sem=recv.at[25 + par],
            device_id={"phi": t},
            device_id_type=MESH,
        )

    def own_copy(par):
        return pltpu.make_async_copy(
            v1.at[par, block(phi)], w_ref.at[:, phi, pl.ds(par * HALF, HALF)], keep_sem.at[par]
        )

    def send_quarter(par, piece):
        for n in range(4):
            t = piece * 4 + lax.rem(phi + n, 4)

            @pl.when(t != phi)
            def _():
                last_copy(par, t).start()

    for par in range(2):

        def backward(m, carry):
            fourth.wait_recv_mode(par, par * FEW + m)
            for b in range(GROUP):
                p2[par, pl.ds(pl.multiple_of(m * (GROUP * GROUP) + b * GROUP, GROUP), GROUP), :] = p3[
                    par, pl.ds(m * GROUP + b, GROUP, stride=BLOCK), :
                ]
            fifth.start_mode(par, m, par)
            return carry

        lax.fori_loop(0, FEW, backward, 0)
        fifth.keep(par)
        fifth.wait_recv(par)
        hartley(
            bh, bl, q1, v1, par, order[2 + par], xs, phi // 4, lambda piece: send_quarter(par, piece)
        )
        own_copy(par).start()

    others = sc.at[pl.ds(0, GROUP - 1)]
    all_scales = scale_copy(others, others, lax.rem(gz + 1, GROUP))
    all_scales.wait_recv()
    total = sc[0]
    for n in range(1, GROUP):
        total = total + sc[n]
    s_ref[...] = total[:VCYC, :BLOCK]

    for exchange in (first, second, third, fourth, fifth):
        for par in range(2):
            exchange.wait_send(par)
    all_scales.wait_send()
    for par in range(2):
        sixth.wait_recv(par)
        sixth.wait_send(par)
        own_copy(par).wait()


def run(charge, outer, end, tables):
    rows = lambda: pltpu.VMEM((2, NPHI, HALF), f32)
    quad = lambda n: pltpu.VMEM((n, HALF, HALF), f32)
    table = lambda: pltpu.VMEM((NPHI, NPHI), bf16)
    whole = pl.BlockSpec(memory_space=pltpu.VMEM)
    away = pl.BlockSpec(memory_space=pl.ANY)
    return pl.pallas_call(
        main_kernel,
        out_shape=(
            jax.ShapeDtypeStruct((BLOCK, GROUP, NR), f32),
            jax.ShapeDtypeStruct((VCYC, BLOCK), f32),
        ),
        in_specs=[away] * 7,
        out_specs=(away, whole),
        scratch_shapes=[
            pltpu.VMEM((1, NZ), jnp.int32),
            pltpu.VMEM((1, NR), jnp.int32),
            *[rows() for _ in range(10)],
            pltpu.VMEM((4, HALF, HALF), bf16),
            pltpu.VMEM((NPHI, NR), bf16),
            table(), table(), table(), table(),
            quad(4), quad(5), quad(5), quad(4),
            pltpu.VMEM((4, HALF + 2 * PAD, HALF), f32),
            pltpu.VMEM((4, HALF + 2 * PAD, HALF), f32),
            quad(4),
            pltpu.VMEM((HALF + 2 * PAD, HALF), f32),
            pltpu.VMEM((HALF + 2 * PAD, HALF), f32),
            pltpu.VMEM((HALF, HALF), f32),
            pltpu.VMEM((8, HALF), f32),
            pltpu.VMEM((GROUP, 8, HALF), f32),
            pltpu.SemaphoreType.DMA((2,)),
            pltpu.SemaphoreType.DMA((6,)),
            pltpu.SemaphoreType.DMA((2,)),
            pltpu.SemaphoreType.DMA((6, 2)),
            pltpu.SemaphoreType.DMA((27,)),
            pltpu.SemaphoreType.DMA,
            pltpu.SemaphoreType.DMA,
        ],
        compiler_params=pltpu.CompilerParams(
            collective_id=0, has_side_effects=True, vmem_limit_bytes=62 << 20
        ),
        name="modes",
    )(charge, outer, end, *tables)


def body(tables, charge, outer_held, end_held):
    hartleys = tuple(jnp.asarray(t) for t in tables)
    w, scales = run(charge, outer_held.reshape(1, NZ), end_held.reshape(1, NR), hartleys)
    return (w, scales)


def solution(mesh):
    in_specs = (P("phi", "gz", None), P(), P())
    out_specs = (P("phi", "gz", None), P(None, "phi"))
    return jax.shard_map(
        functools.partial(body, hartley_tables()),
        mesh=mesh,
        in_specs=in_specs,
        out_specs=out_specs,
        check_vma=False,
    )
```

```python
import functools
import math

import jax
import jax.numpy as jnp
import numpy as np
from jax import lax
from jax.experimental import pallas as pl
from jax.experimental.pallas import tpu as pltpu
from jax.sharding import PartitionSpec as P

NPHI = 1024
VCYC = 2
NU = 2
KC = 3
RIN = 131
NR = 256
NZ = 256
HALF = 128
FEW = 4
GROUP = 16
BLOCK = 64
MESH = pl.DeviceIdType.MESH

relaxation = 0.8
small_floor = 1e-06
f32 = jnp.float32
bf16 = jnp.bfloat16

PAD = 8
CH = 32


def hartley_tables():
    k = np.arange(NPHI)
    phase = (np.outer(k, k) % NPHI) * (2.0 * math.pi / NPHI)
    table = ((np.cos(phase) + np.sin(phase)) / math.sqrt(NPHI)).astype(np.float32)
    order = k.reshape(GROUP, GROUP, FEW).transpose(2, 1, 0).reshape(-1)
    table = table[order]
    high = table.astype(jnp.bfloat16)
    low = (table - high.astype(np.float32)).astype(jnp.bfloat16)
    return high, low, np.ascontiguousarray(high.T), np.ascontiguousarray(low.T)


def split(values):
    high = values.astype(bf16)
    low = (values - high.astype(f32)).astype(bf16)
    return high, low


def lane_ids(rows=1):
    return lax.broadcasted_iota(jnp.int32, (rows, HALF), 1)


def fine_rows(parity):
    i = 2 * lane_ids() + parity
    radius = i.astype(f32) + (RIN + 0.5)
    inward = (radius - 0.5) / radius
    outward = (radius + 0.5) / radius
    return radius, inward, outward


def coarse_rows():
    radius = 2.0 * lane_ids().astype(f32) + (RIN + 1.0)
    inward = (radius - 1.0) / (4.0 * radius)
    outward = (radius + 1.0) / (4.0 * radius)
    return radius, inward, outward


def as_column(row):
    square = jnp.broadcast_to(row, (HALF, HALF))
    diag = lax.broadcasted_iota(jnp.int32, (HALF, HALF), 0) == lane_ids(HALF)
    return jnp.sum(jnp.where(diag, square, 0.0), axis=1, keepdims=True)


def setup_base(base_ref, outer_rows, end_rows):
    y = lax.broadcasted_iota(jnp.int32, (HALF, HALF), 0)
    j = lane_ids(HALF)
    for zp in range(2):
        open_outer = 1.0 - as_column(outer_rows[zp])
        for ip in range(2):
            _, inward, outward = fine_rows(ip)
            open_end = 1.0 - end_rows[ip]
            value = jnp.broadcast_to(inward + outward + 2.0, (HALF, HALF))
            if ip == 1:
                value = value - jnp.where(j == HALF - 1, outward * open_outer, 0.0)
            edge = 0 if zp == 0 else HALF - 1
            value = value - jnp.where(y == edge, open_end, 0.0)
            base_ref[2 * zp + ip] = value
    _, inward, outward = coarse_rows()
    open_outer = 1.0 - as_column(outer_rows[0])
    open_end = 1.0 - end_rows[0]
    value = jnp.broadcast_to(inward + outward + 0.5, (HALF, HALF))
    value = value - jnp.where(j == HALF - 1, outward * open_outer, 0.0)
    value = value - jnp.where((y == 0) | (y == HALF - 1), 0.25 * open_end, 0.0)
    base_ref[4] = value


def parity_matrix(half):
    cell = lax.broadcasted_iota(jnp.int32, (HALF, HALF), 0)
    lane = lax.broadcasted_iota(jnp.int32, (HALF, HALF), 1)
    second = (cell % 2) != half
    target = cell // 2 + jnp.where(second, HALF // 2, 0)
    return jnp.where(lane == target, 1.0, 0.0)


def even_odd(first, second):
    low = lane_ids(first.shape[0]) < HALF // 2
    even = jnp.where(low, first, second)
    odd = pltpu.roll(jnp.where(low, second, first), HALF // 2, 1)
    return even, odd


def two_halves(even, odd):
    low = lane_ids(even.shape[0]) < HALF // 2
    odd = pltpu.roll(odd, HALF // 2, 1)
    return jnp.where(low, even, odd), jnp.where(low, odd, even)


def left_of(value):
    return pltpu.roll(value, 1, 1)


def right_of(value):
    return pltpu.roll(value, HALF - 1, 1)


def solve_mode(mode, f_ref, base_ref, d_ref, w_ref, va, vb, r_ref, ca, cb, cr_ref, write):
    order = jnp.minimum(mode, NPHI - mode).astype(f32)
    square = order * order
    rows_e = fine_rows(0)
    rows_o = fine_rows(1)
    first = lane_ids() == 0
    last = lane_ids() == HALF - 1
    in_e = jnp.where(first, 0.0, rows_e[1])
    out_e = rows_e[2]
    in_o = rows_o[1]
    out_o = jnp.where(last, 0.0, rows_o[2])
    radius_c, in_c0, out_c0 = coarse_rows()
    in_c = jnp.where(first, 0.0, in_c0)
    out_c = jnp.where(last, 0.0, out_c0)
    term_e = square / (rows_e[0] * rows_e[0])
    term_o = square / (rows_o[0] * rows_o[0])
    term_c = square / (radius_c * radius_c)
    chunks = [pl.ds(s, CH) for s in range(0, HALF, CH)]
    padded = [pl.ds(PAD + s, CH) for s in range(0, HALF, CH)]
    above = [pl.ds(PAD + s - 1, CH) for s in range(0, HALF, CH)]
    below = [pl.ds(PAD + s + 1, CH) for s in range(0, HALF, CH)]
    count = len(chunks)

    def neighbours(v, c):
        ee, eo, oe, oo = (v[q, padded[c], :] for q in range(4))
        oe_up, oo_up = v[2, above[c], :], v[3, above[c], :]
        ee_dn, eo_dn = v[0, below[c], :], v[1, below[c], :]
        n_ee = (oe_up + oe) + (in_e * left_of(eo) + out_e * eo)
        n_eo = (oo_up + oo) + (in_o * ee + out_o * right_of(ee))
        n_oe = (ee + ee_dn) + (in_e * left_of(oo) + out_e * oo)
        n_oo = (eo + eo_dn) + (in_o * oe + out_o * right_of(oe))
        return (ee, eo, oe, oo), (n_ee, n_eo, n_oe, n_oo)

    def sweep(src, dst, emit=None):
        for c in range(count):
            centre, near = neighbours(src, c)
            values = []
            for q in range(4):
                value = (1.0 - relaxation) * centre[q] + w_ref[q, chunks[c], :] * (
                    f_ref[q, chunks[c], :] + near[q]
                )
                if emit is None:
                    dst[q, padded[c], :] = value
                values.append(value)
            if emit is not None:
                emit(c * CH, values)

    for c in range(count):
        for q in range(4):
            d = base_ref[q, chunks[c], :] + (term_e if q % 2 == 0 else term_o)
            w = relaxation / d
            d_ref[q, chunks[c], :] = d
            w_ref[q, chunks[c], :] = w
            va[q, padded[c], :] = w * f_ref[q, chunks[c], :]
        d_ref[4, chunks[c], :] = relaxation / (base_ref[4, chunks[c], :] + term_c)

    factors = []
    cur, other = va, vb
    for cycle in range(VCYC):
        for s in range(1 if cycle == 0 else 0, NU):
            sweep(cur, other)
            cur, other = other, cur
        for c in range(count):
            centre, near = neighbours(cur, c)
            total = None
            for q in range(4):
                res = f_ref[q, chunks[c], :] + near[q] - d_ref[q, chunks[c], :] * centre[q]
                r_ref[q, chunks[c], :] = res
                total = res if total is None else total + res
            total = total * 0.25
            cr_ref[chunks[c], :] = total
            ca[padded[c], :] = d_ref[4, chunks[c], :] * total
        now, later = ca, cb
        for s in range(KC):
            for c in range(count):
                w = now[padded[c], :]
                near = (
                    in_c * left_of(w)
                    + out_c * right_of(w)
                    + 0.25 * (now[above[c], :] + now[below[c], :])
                )
                later[padded[c], :] = (1.0 - relaxation) * w + d_ref[4, chunks[c], :] * (
                    cr_ref[chunks[c], :] + near
                )
            now, later = later, now
        top = jnp.zeros((8, HALF), f32)
        bottom = jnp.zeros((8, HALF), f32)
        for c in range(count):
            w = now[padded[c], :]
            low_e = in_e * left_of(w) + out_e * w
            low_o = in_o * w + out_o * right_of(w)
            up = now[above[c], :] + w
            down = now[below[c], :] + w
            for q in range(4):
                image = d_ref[q, chunks[c], :] * w - (low_e if q % 2 == 0 else low_o)
                image = image - (up if q < 2 else down)
                res = r_ref[q, chunks[c], :]
                for g in range(CH // 8):
                    part = image[8 * g : 8 * g + 8]
                    top = top + res[8 * g : 8 * g + 8] * part
                    bottom = bottom + part * part
        factor = jnp.sum(top, keepdims=True) / (jnp.sum(bottom, keepdims=True) + small_floor)
        factors.append(factor)
        for c in range(count):
            add = factor * now[padded[c], :]
            for q in range(4):
                cur[q, padded[c], :] = cur[q, padded[c], :] + add
        for s in range(NU):
            if cycle == VCYC - 1 and s == NU - 1:
                sweep(cur, None, write)
            else:
                sweep(cur, other)
                cur, other = other, cur
    return factors


def block(index):
    return pl.ds(pl.multiple_of(index * BLOCK, BLOCK), BLOCK)


def far_peers(me, action):
    def step(n, carry):
        away = (GROUP // 2 - (n + 1) // 2) * (1 - 2 * lax.rem(n, 2))
        action(lax.rem(me + GROUP + away, GROUP))
        return carry

    lax.fori_loop(0, GROUP - 1, step, 0)


def peers(me, action):
    def step(n, carry):
        away = (n // 2 + 1) * (1 - 2 * lax.rem(n, 2))
        action(lax.rem(me + GROUP + away, GROUP))
        return carry

    lax.fori_loop(0, GROUP - 1, step, 0)


class Exchange:
    def __init__(self, axis, src, dst, send, recv, base, by_mode=False):
        self.axis, self.src, self.dst, self.send, self.recv = axis, src, dst, send, recv
        self.base, self.by_mode = base, by_mode
        self.me = lax.axis_index(axis)

    def copy(self, par, source, target, t, sem):
        return pltpu.make_async_remote_copy(
            src_ref=self.src.at[par, source],
            dst_ref=self.dst.at[par, target],
            send_sem=self.send,
            recv_sem=self.recv.at[self.base + sem],
            device_id={self.axis: t},
            device_id_type=MESH,
        )

    def place(self, t, m):
        if self.by_mode:
            return pl.ds(pl.multiple_of(m * (GROUP * GROUP) + t * GROUP, GROUP), GROUP)
        return pl.ds(pl.multiple_of(t * BLOCK + m * GROUP, GROUP), GROUP)

    def start(self, par, t):
        self.copy(par, block(t), block(self.me), t, par).start()

    def start_mode(self, par, m, sem):
        peers(
            self.me,
            lambda t: self.copy(par, self.place(t, m), self.place(self.me, m), t, sem).start(),
        )

    def keep(self, par):
        for m in range(FEW):
            here = self.place(self.me, m)
            self.dst[par, here, :] = self.src[par, here, :]

    def whole(self, par, rows, sem):
        t = lax.rem(self.me + 1, GROUP)
        return self.copy(par, pl.ds(0, rows), pl.ds(0, rows), t, sem)

    def wait_recv(self, par):
        self.whole(par, (GROUP - 1) * BLOCK, par).wait_recv()

    def wait_recv_mode(self, par, sem):
        self.whole(par, (GROUP - 1) * GROUP, sem).wait_recv()

    def wait_send(self):
        rows = pl.ds(0, (GROUP - 1) * BLOCK)
        self.copy(slice(None), rows, rows, lax.rem(self.me + 1, GROUP), 0).wait_send()


def hartley(high, low, src, dst, par, order, xs, first, ready):
    for piece in range(4):
        rows = pl.ds(piece * 256, 256)
        h, l = split(src[par, rows, :])
        xs[rows, :HALF] = jnp.dot(h, order, preferred_element_type=f32).astype(bf16)
        xs[rows, HALF:] = jnp.dot(l, order, preferred_element_type=f32).astype(bf16)
    def step(n, carry):
        piece = lax.rem(first + n, 4)
        rows = pl.ds(pl.multiple_of(piece * 256, 256), 256)
        both = jnp.dot(high[rows, :], xs[...], preferred_element_type=f32)
        rest = jnp.dot(low[rows, :], xs[:, :HALF], preferred_element_type=f32)
        dst[par, rows, :] = both[:, :HALF] + (both[:, HALF:] + rest)
        ready(piece)
        return carry

    lax.fori_loop(0, 4, step, 0)


def main_kernel(
    charge_ref, outer_ref, end_ref, fh_ref, fl_ref, bh_ref, bl_ref,
    w_ref, s_ref,
    outer, end, r1, s1, r2, r3, r4, o4, p3, p2, q1, v1, order, xs,
    fh, fl, bh, bl,
    f, base, d, w, va, vb, r, ca, cb, cr, sc_src, sc,
    in_sem, table_sem, keep_sem, send, recv, sc_send, sc_recv,
):
    phi, gz = lax.axis_index("phi"), lax.axis_index("gz")
    own_loads = [
        pltpu.make_async_copy(
            charge_ref.at[:, phi, pl.ds(half * HALF, HALF)], r1.at[half, block(phi)], in_sem.at[half]
        )
        for half in range(2)
    ]
    tables = [
        pltpu.make_async_copy(src, dst, table_sem.at[n])
        for n, (src, dst) in enumerate(((outer_ref, outer), (end_ref, end), (fh_ref, fh), (fl_ref, fl), (bh_ref, bh), (bl_ref, bl)))
    ]
    barrier = pltpu.get_barrier_semaphore()
    for axis, me in (("phi", phi), ("gz", gz)):
        peers(
            me,
            lambda t: pl.semaphore_signal(barrier, inc=1, device_id={axis: t}, device_id_type=MESH),
        )

    first = Exchange("phi", s1, r1, send.at[0], recv, 0)
    second = Exchange("gz", s1, r2, send.at[1], recv, 2, True)
    third = Exchange("phi", r3, r4, send.at[2], recv, 10)
    fourth = Exchange("phi", o4, p3, send.at[3], recv, 15)
    fifth = Exchange("gz", p2, q1, send.at[4], recv, 23, True)
    sixth = Exchange("phi", v1, q1, send.at[5], recv, 25)

    pl.semaphore_wait(barrier, 2 * (GROUP - 1))

    def first_copy(half, t):
        return pltpu.make_async_remote_copy(
            src_ref=charge_ref.at[:, t, pl.ds(half * HALF, HALF)],
            dst_ref=r1.at[half, block(phi)],
            send_sem=send.at[0],
            recv_sem=recv.at[half],
            device_id={"phi": t},
            device_id_type=MESH,
        )

    for half in range(2):
        far_peers(phi, lambda t: first_copy(half, t).start())
        own_loads[half].start()
    for copy in tables:
        copy.start()

    for copy in tables:
        copy.wait()
    orders = [parity_matrix(0), parity_matrix(1)]
    held = jnp.concatenate([outer[...]] * 4 + [end[...]] * 4, axis=0).astype(f32)
    held = even_odd(*(
        jnp.dot(
            held[:, n * HALF : (n + 1) * HALF].astype(bf16),
            orders[n].astype(bf16),
            preferred_element_type=f32,
        )
        for n in range(2)
    ))
    setup_base(base, [row[0:1] for row in held], [row[4:5] for row in held])
    for n in range(2):
        order[n] = orders[n].astype(bf16)
        order[2 + n] = jnp.transpose(orders[n]).astype(bf16)
    for ref in (va, vb):
        ref[:, 0:PAD, :] = jnp.zeros((4, PAD, HALF), f32)
        ref[:, HALF + PAD :, :] = jnp.zeros((4, PAD, HALF), f32)
    for ref in (ca, cb):
        ref[0:PAD, :] = jnp.zeros((PAD, HALF), f32)
        ref[HALF + PAD :, :] = jnp.zeros((PAD, HALF), f32)
    sc_src[...] = jnp.zeros((8, HALF), f32)

    for par in range(2):
        first.wait_recv(par)
        own_loads[par].wait()
        hartley(
            fh, fl, r1, s1, par, order[par], xs, 0,
            lambda m: second.start_mode(par, m, par * FEW + m),
        )
        second.keep(par)

        def forward(m, carry):
            second.wait_recv_mode(par, par * FEW + m)
            for b in range(GROUP):
                r3[par, pl.ds(m * GROUP + b, GROUP, stride=BLOCK), :] = r2[
                    par, pl.ds(pl.multiple_of(m * (GROUP * GROUP) + b * GROUP, GROUP), GROUP), :
                ]
            third.start_mode(par, m, par * (1 + m))
            return carry

        lax.fori_loop(0, FEW, forward, 0)
        third.keep(par)

    third.wait_recv(0)

    def solve_step(m, carry):
        third.wait_recv_mode(1, 1 + m)
        mode = (phi * GROUP + gz) * FEW + m
        rows = lambda zp, b: pl.ds(zp * BLOCK + m * GROUP + b, 8, stride=HALF)
        for zp in range(2):
            for b in range(GROUP):
                even, odd = even_odd(r4[0, rows(zp, b), :], r4[1, rows(zp, b), :])
                f[2 * zp, 8 * b : 8 * b + 8, :] = even
                f[2 * zp + 1, 8 * b : 8 * b + 8, :] = odd

        def write(start, values):
            for zp in range(2):
                halves = two_halves(values[2 * zp], values[2 * zp + 1])
                for g in range(CH // 8):
                    for n in range(2):
                        o4[n, rows(zp, start // 8 + g), :] = halves[n][8 * g : 8 * g + 8]

        factors = solve_mode(mode, f, base, d, w, va, vb, r, ca, cb, cr, write)
        row_ids = lax.broadcasted_iota(jnp.int32, (8, HALF), 0)
        lanes = lane_ids(8)
        for cycle in range(VCYC):
            here = (row_ids == cycle) & (lanes == gz * FEW + m)
            sc_src[...] = sc_src[...] + jnp.where(here, factors[cycle], 0.0)
        fourth.start_mode(0, m, m)
        return carry

    lax.fori_loop(0, FEW, solve_step, 0)

    for m in range(FEW):
        fourth.start_mode(1, m, FEW + m)
    fourth.keep(0)
    fourth.keep(1)

    def scale_copy(source, target, t):
        return pltpu.make_async_remote_copy(
            src_ref=source,
            dst_ref=target,
            send_sem=sc_send,
            recv_sem=sc_recv,
            device_id={"gz": t},
            device_id_type=MESH,
        )

    peers(gz, lambda t: scale_copy(sc_src, sc.at[gz], t).start())
    sc[gz] = sc_src[...]

    def last_copy(par, t):
        return pltpu.make_async_remote_copy(
            src_ref=v1.at[par, block(t)],
            dst_ref=w_ref.at[:, phi, pl.ds(par * HALF, HALF)],
            send_sem=send.at[5],
            recv_sem=recv.at[25 + par],
            device_id={"phi": t},
            device_id_type=MESH,
        )

    def own_copy(par):
        return pltpu.make_async_copy(
            v1.at[par, block(phi)], w_ref.at[:, phi, pl.ds(par * HALF, HALF)], keep_sem.at[par]
        )

    def send_quarter(par, piece):
        for n in range(4):
            t = piece * 4 + lax.rem(phi + n, 4)

            @pl.when(t != phi)
            def _():
                last_copy(par, t).start()

    for par in range(2):

        def backward(m, carry):
            fourth.wait_recv_mode(par, par * FEW + m)
            for b in range(GROUP):
                p2[par, pl.ds(pl.multiple_of(m * (GROUP * GROUP) + b * GROUP, GROUP), GROUP), :] = p3[
                    par, pl.ds(m * GROUP + b, GROUP, stride=BLOCK), :
                ]
            fifth.start_mode(par, m, par)
            return carry

        lax.fori_loop(0, FEW, backward, 0)
        fifth.keep(par)
        fifth.wait_recv(par)
        hartley(
            bh, bl, q1, v1, par, order[2 + par], xs, phi // 4, lambda piece: send_quarter(par, piece)
        )
        own_copy(par).start()

    others = sc.at[pl.ds(0, GROUP - 1)]
    all_scales = scale_copy(others, others, lax.rem(gz + 1, GROUP))
    all_scales.wait_recv()
    total = sc[0]
    for n in range(1, GROUP):
        total = total + sc[n]
    s_ref[...] = total[:VCYC, :BLOCK]

    for exchange in (first, second, third, fourth, fifth):
        exchange.wait_send()
    all_scales.wait_send()
    for par in range(2):
        sixth.wait_recv(par)
        own_copy(par).wait()
    sixth.wait_send()


def run(charge, outer, end, tables):
    rows = lambda: pltpu.VMEM((2, NPHI, HALF), f32)
    quad = lambda n: pltpu.VMEM((n, HALF, HALF), f32)
    table = lambda: pltpu.VMEM((NPHI, NPHI), bf16)
    whole = pl.BlockSpec(memory_space=pltpu.VMEM)
    away = pl.BlockSpec(memory_space=pl.ANY)
    return pl.pallas_call(
        main_kernel,
        out_shape=(
            jax.ShapeDtypeStruct((BLOCK, GROUP, NR), f32),
            jax.ShapeDtypeStruct((VCYC, BLOCK), f32),
        ),
        in_specs=[away] * 7,
        out_specs=(away, whole),
        scratch_shapes=[
            pltpu.VMEM((1, NZ), jnp.int32),
            pltpu.VMEM((1, NR), jnp.int32),
            *[rows() for _ in range(10)],
            pltpu.VMEM((4, HALF, HALF), bf16),
            pltpu.VMEM((NPHI, NR), bf16),
            table(), table(), table(), table(),
            quad(4), quad(5), quad(5), quad(4),
            pltpu.VMEM((4, HALF + 2 * PAD, HALF), f32),
            pltpu.VMEM((4, HALF + 2 * PAD, HALF), f32),
            quad(4),
            pltpu.VMEM((HALF + 2 * PAD, HALF), f32),
            pltpu.VMEM((HALF + 2 * PAD, HALF), f32),
            pltpu.VMEM((HALF, HALF), f32),
            pltpu.VMEM((8, HALF), f32),
            pltpu.VMEM((GROUP, 8, HALF), f32),
            pltpu.SemaphoreType.DMA((2,)),
            pltpu.SemaphoreType.DMA((6,)),
            pltpu.SemaphoreType.DMA((2,)),
            pltpu.SemaphoreType.DMA((6,)),
            pltpu.SemaphoreType.DMA((27,)),
            pltpu.SemaphoreType.DMA,
            pltpu.SemaphoreType.DMA,
        ],
        compiler_params=pltpu.CompilerParams(
            collective_id=0, has_side_effects=True, vmem_limit_bytes=62 << 20
        ),
        name="modes",
    )(charge, outer, end, *tables)


def finish_kernel(w_ref, o_ref, held, load_sem, store_sem):
    loads, stores = [], []
    for n in range(4):
        rows = pl.ds(GROUP * n, GROUP)
        loads.append(pltpu.make_async_copy(w_ref.at[rows], held.at[rows], load_sem.at[n]))
        stores.append(pltpu.make_async_copy(held.at[rows], o_ref.at[rows], store_sem.at[n]))
    for copy in loads:
        copy.start()
    for load, store in zip(loads, stores):
        load.wait()
        store.start()
    for copy in stores:
        copy.wait()


def finish(w):
    return pl.pallas_call(
        finish_kernel,
        out_shape=jax.ShapeDtypeStruct((BLOCK, GROUP, NR), f32),
        in_specs=[pl.BlockSpec(memory_space=pltpu.HBM)],
        out_specs=pl.BlockSpec(memory_space=pltpu.HBM),
        scratch_shapes=[
            pltpu.VMEM((BLOCK, GROUP, NR), f32),
            pltpu.SemaphoreType.DMA((4,)),
            pltpu.SemaphoreType.DMA((4,)),
        ],
        compiler_params=pltpu.CompilerParams(vmem_limit_bytes=63 << 20),
        name="finish",
    )(w)


def body(tables, charge, outer_held, end_held):
    hartleys = tuple(jnp.asarray(t) for t in tables)
    w, scales = run(charge, outer_held.reshape(1, NZ), end_held.reshape(1, NR), hartleys)
    return (finish(w), scales)


def solution(mesh):
    in_specs = (P("phi", "gz", None), P(), P())
    out_specs = (P("phi", "gz", None), P(None, "phi"))
    return jax.shard_map(
        functools.partial(body, hartley_tables()),
        mesh=mesh,
        in_specs=in_specs,
        out_specs=out_specs,
        check_vma=False,
    )
```
